32 devices in a mesh: row: 8 (over y, x, core), col: 4 (over z).
Axes of the slice: x: 2, y: 2, z: 4, core: 2. Of those that a mesh axis runs over, the one named last changes fastest.
Arguments:
- upper_blocks: bfloat16 [64, 8, 128, 128], P('row', None, 'col'), as said below
- block_cols: int32 [64, 8], replicated, may hold values from -1 to 63, as said below
- filter_cols: int32 [64, 8], replicated, may hold values from -1 to 63, as said below
Outputs:
- purified: float32 [64, 8, 128, 128], P('row', None, 'col')
The draws below stay inside these ranges and needn't reach their ends.
Inputs may be any that keep to these rules, and one draw needn't show every extreme that they name: `block_cols`: slot 0 of row i holds i; every other slot holds -1 or a block column j with i < j < i + 8 and j < 64; the columns of a row are distinct; rows i <= 56 have no -1. `filter_cols`: slot 0 of row i holds i; every other slot holds -1 or a block column j with i < j < i + 8 and j < 64; the columns of a row are distinct; rows i <= 56 have no -1. Every diagonal block upper_blocks[i, 0] is symmetric.
All inputs are finite; a program needn't handle non-finite values.
Results may differ from the reference program's by a relative error of at most 0.002.
Values may be sent and summed in bfloat16 or wider, within the bound.
A program may use at most 128 MiB of HBM per device.

```python
import jax
import jax.numpy as jnp
from jax import lax

B = 128
W = 8
K = 8
KF = 8
NB = 64


def pattern_draw(key, slots):
    row_labels = jnp.arange(NB, dtype=jnp.int32)[:, None]
    offsets = jnp.arange(1, W, dtype=jnp.int32)[None, :]
    scores = jax.random.randint(key, (NB, W - 1), 0, 1 << 20, dtype=jnp.int32) * W + offsets
    ordering = jnp.argsort(scores, axis=1)
    chosen = ordering[:, :slots - 1].astype(jnp.int32) + 1 + row_labels
    chosen = jnp.where(chosen < NB, chosen, -1)
    return jnp.concatenate([row_labels, chosen], axis=1).astype(jnp.int32)


def draw_block_cols(key, part):
    return pattern_draw(jax.random.fold_in(key, 11), K)


def draw_filter_cols(key, part):
    return pattern_draw(jax.random.fold_in(key, 23), KF)


def draw_upper_blocks(key, part):
    values = jax.random.normal(key, (NB, K, B, B), jnp.float32)
    symmetric = (values + jnp.swapaxes(values, 2, 3)) * 0.70710678
    slot_labels = jnp.arange(K, dtype=jnp.int32)[None, :, None, None]
    values = jnp.where(slot_labels == 0, symmetric, values)
    return (0.1 * values).astype(jnp.bfloat16)


def setup_inputs(seed: int = 0) -> dict:
    keys = jax.random.split(jax.random.key(seed), 4)
    upper_blocks = draw_upper_blocks(jax.random.fold_in(keys[3], 71), 0)
    block_cols = draw_block_cols(jax.random.fold_in(keys[3], 71), 0)
    filter_cols = draw_filter_cols(jax.random.fold_in(keys[3], 71), 0)
    return dict(upper_blocks=upper_blocks, block_cols=block_cols, filter_cols=filter_cols)


row_group = 4


def band_right(blocks, columns, first_row):
    count_rows = blocks.shape[0]
    rim_rows = W - 1
    count_cols = count_rows - rim_rows
    first_col = first_row + rim_rows
    column_ids = first_col + jnp.arange(count_cols, dtype=jnp.int32)
    row_labels = first_row + jnp.arange(count_rows, dtype=jnp.int32)
    upper_hit = (columns[:, :, None] == column_ids[None, None, :]).astype(jnp.float32)
    upper_part = jnp.einsum("akxy,akb->axby", blocks.astype(jnp.float32), upper_hit)
    source = columns[rim_rows:]
    lower_hit = (source[:, :, None] == row_labels[None, None, :]) & (source[:, :, None] > column_ids[:, None, None])
    lower_part = jnp.einsum("bkxy,bka->aybx", blocks[rim_rows:].astype(jnp.float32), lower_hit.astype(jnp.float32))
    return (upper_part + lower_part).astype(jnp.bfloat16)


def left_from_filter(own_slots, own_targets, mirror_slots, mirror_targets, first_row, row_count):
    rim_rows = W - 1
    count_cols = row_count + 2 * rim_rows
    band_ids = first_row + jnp.arange(count_cols, dtype=jnp.int32)
    own_ids = first_row + rim_rows + jnp.arange(row_count, dtype=jnp.int32)
    upper_hit = (own_targets[:, :, None] == band_ids[None, None, :]).astype(jnp.float32)
    upper_part = jnp.einsum("ifxy,ifa->ixay", own_slots.astype(jnp.float32), upper_hit)
    mirror_ids = first_row + jnp.arange(row_count + rim_rows, dtype=jnp.int32)
    lower_hit = (mirror_targets[:, :, None] == own_ids[None, None, :]) & (mirror_targets[:, :, None] > mirror_ids[:, None, None])
    lower_part = jnp.einsum("mfxy,mfi->ixmy", mirror_slots.astype(jnp.float32), lower_hit.astype(jnp.float32))
    lower_part = jnp.pad(lower_part, ((0, 0), (0, 0), (0, rim_rows), (0, 0)))
    return (upper_part + lower_part).astype(jnp.bfloat16)


def pick_slots(product, targets, first_col):
    column_ids = first_col + jnp.arange(product.shape[2], dtype=jnp.int32)
    selector = (targets[:, :, None] == column_ids[None, None, :]).astype(jnp.float32)
    return jnp.einsum("ixby,ifb->ifxy", product, selector, precision=lax.Precision.HIGHEST)


def group_products(left_rows, right_band, targets, first_col):
    outputs = []
    row_count = left_rows.shape[0]
    inner_rows = left_rows.shape[1]
    span_rows = row_group + 2 * (W - 1)
    width_cols = row_group + W - 1
    for group_index in range(row_count // row_group):
        row_start = group_index * row_group
        left_part = left_rows[row_start:row_start + row_group, :, row_start:row_start + span_rows, :]
        left_part = left_part.reshape(row_group * inner_rows, span_rows * B)
        right_part = right_band[row_start:row_start + span_rows, :, row_start:row_start + width_cols, :]
        right_part = right_part.reshape(span_rows * B, width_cols * B)
        product = jnp.dot(left_part, right_part, preferred_element_type=jnp.float32)
        product = product.reshape(row_group, inner_rows, width_cols, B)
        outputs.append(pick_slots(product, targets[row_start:row_start + row_group], first_col + row_start))
    return jnp.concatenate(outputs, axis=0)


def reference(upper_blocks, block_cols, filter_cols):
    rim_rows = W - 1
    group_count = NB // row_group
    padded_blocks = jnp.pad(upper_blocks, ((rim_rows, rim_rows), (0, 0), (0, 0), (0, 0)))
    padded_cols = jnp.pad(block_cols, ((rim_rows, rim_rows), (0, 0)), constant_values=-1)
    padded_filter = jnp.pad(filter_cols, ((rim_rows, 0), (0, 0)), constant_values=-1)

    def window_band(row_first):
        window_blocks = lax.dynamic_slice_in_dim(padded_blocks, row_first, row_group + 2 * rim_rows, 0)
        window_cols = lax.dynamic_slice_in_dim(padded_cols, row_first, row_group + 2 * rim_rows, 0)
        return band_right(window_blocks, window_cols, row_first - rim_rows)

    def square_group(group_index):
        row_first = (group_index * row_group).astype(jnp.int32)
        right_band = window_band(row_first)
        left_rows = jnp.transpose(right_band[:, :, :row_group, :], (2, 3, 0, 1))
        own_filter = lax.dynamic_slice_in_dim(filter_cols, row_first, row_group, 0)
        return group_products(left_rows, right_band, own_filter, row_first)

    group_ids = jnp.arange(group_count, dtype=jnp.int32)
    square = lax.map(square_group, group_ids).reshape(NB, KF, B, B)
    square_half = square.astype(jnp.bfloat16)
    padded_half = jnp.pad(square_half, ((rim_rows, 0), (0, 0), (0, 0), (0, 0)))

    def cube_group(group_index):
        row_first = (group_index * row_group).astype(jnp.int32)
        right_band = window_band(row_first)
        own_filter = lax.dynamic_slice_in_dim(filter_cols, row_first, row_group, 0)
        own_slots = lax.dynamic_slice_in_dim(square_half, row_first, row_group, 0)
        mirror_slots = jnp.swapaxes(lax.dynamic_slice_in_dim(padded_half, row_first, row_group + rim_rows, 0), 2, 3)
        mirror_targets = lax.dynamic_slice_in_dim(padded_filter, row_first, row_group + rim_rows, 0)
        left_filter = left_from_filter(own_slots, own_filter, mirror_slots, mirror_targets, row_first - rim_rows, row_group)
        return group_products(left_filter, right_band, own_filter, row_first)

    cube_terms = lax.map(cube_group, group_ids).reshape(NB, KF, B, B)
    return 3.0 * square - 2.0 * cube_terms
```

```python
import functools

import jax
import jax.numpy as jnp
from jax import lax
from jax.experimental import pallas as pl
from jax.experimental.pallas import tpu as pltpu
from jax.sharding import PartitionSpec as P

B = 128
W = 8
RIM = W - 1
MESH = pl.DeviceIdType.MESH
NT = (((1,), (1,)), ((), ()))


def band_kernel(cols, slots, out):
    rows, kinds = slots.shape[0], slots.shape[1]
    first = lax.axis_index("row") * rows
    out[...] = jnp.zeros_like(out)
    for i in range(rows):
        for k in range(kinds):
            column = cols[first + i, k]

            @pl.when(column >= 0)
            def _(i=i, k=k, column=column):
                out[i, column - first - i] = slots[i, k]


def gather_kernel(
    row_devices, col_devices, own, window, local_sem, col_send, col_recv, row_send, row_recv
):
    rows = own.shape[0]
    r, q = lax.axis_index("row"), lax.axis_index("col")
    has_next, has_before = r < row_devices - 1, r > 0
    has_up, has_down = q < col_devices - 1, q > 0
    next_row, before_row = {"row": r + 1}, {"row": r - 1}
    up_col, down_col = {"col": q + 1}, {"col": q - 1}
    neighbours = (
        (has_next, next_row), (has_before, before_row), (has_up, up_col), (has_down, down_col)
    )

    barrier = pltpu.get_barrier_semaphore()
    count = jnp.int32(0)
    for present, device in neighbours:

        @pl.when(present)
        def _(device=device):
            pl.semaphore_signal(barrier, inc=1, device_id=device, device_id_type=MESH)

        count = count + present.astype(jnp.int32)
    pl.semaphore_wait(barrier, count)

    local = pltpu.make_async_copy(own, window.at[q, RIM : RIM + rows], local_sem)
    local.start()

    def source(shard, is_own):
        return own if is_own else window.at[shard, RIM : RIM + rows]

    def col_copy(shard, is_own, up, step):
        return pltpu.make_async_remote_copy(
            src_ref=source(shard, is_own),
            dst_ref=window.at[shard, RIM : RIM + rows],
            send_sem=col_send.at[0 if up else 1, step],
            recv_sem=col_recv.at[shard],
            device_id=up_col if up else down_col,
            device_id_type=MESH,
        )

    def halo_copies(shard, is_own, onward):
        src = source(shard, is_own)
        if onward:
            parts = (((rows - RIM, rows), (0, W), 0, 0),)
            device = next_row
        else:
            parts = (
                ((0, 4), (0, RIM), RIM + rows, 1),
                ((4, RIM), (0, 3), RIM + rows + 4, 2),
            )
            device = before_row
        return [
            pltpu.make_async_remote_copy(
                src_ref=src.at[lo:hi, kinds[0] : kinds[1]],
                dst_ref=window.at[shard, place : place + hi - lo, kinds[0] : kinds[1]],
                send_sem=row_send.at[part, shard],
                recv_sem=row_recv.at[part, shard],
                device_id=device,
                device_id_type=MESH,
            )
            for (lo, hi), kinds, place, part in parts
        ]

    def spread(shard, is_own):
        for present, onward in ((has_next, True), (has_before, False)):

            @pl.when(present)
            def _(onward=onward):
                for copy in halo_copies(shard, is_own, onward):
                    copy.start()

    @pl.when(has_up)
    def _():
        col_copy(q, True, True, 0).start()

    @pl.when(has_down)
    def _():
        col_copy(q, True, False, 0).start()

    spread(q, True)

    for step in range(1, col_devices):
        for up in (True, False):
            shard = q - step if up else q + step
            arrives = shard >= 0 if up else shard < col_devices
            onward = has_up if up else has_down

            @pl.when(arrives)
            def _(shard=shard, up=up, onward=onward, step=step):
                col_copy(shard, False, up, step).wait_recv()

                @pl.when(onward)
                def _():
                    col_copy(shard, False, up, step).start()

                spread(shard, False)

    local.wait()
    for step in range(col_devices):
        for up in (True, False):
            shard = q - step if up else q + step
            arrives = shard >= 0 if up else shard < col_devices
            onward = has_up if up else has_down

            @pl.when(arrives & onward)
            def _(shard=shard, up=up, step=step):
                col_copy(shard, step == 0, up, step).wait_send()

    for shard in range(col_devices):

        @pl.when(has_next)
        def _(shard=shard):
            for copy in halo_copies(shard, False, True):
                copy.wait_send()
            for copy in halo_copies(shard, False, False):
                copy.wait_recv()

        @pl.when(has_before)
        def _(shard=shard):
            for copy in halo_copies(shard, False, False):
                copy.wait_send()
            for copy in halo_copies(shard, False, True):
                copy.wait_recv()


def product_kernel(
    row_devices, rows, quarter, targets, keep, window, out, blocks, left, filtered, held, sem
):
    span = rows + 2 * RIM
    devices = B // quarter
    r, q = lax.axis_index("row"), lax.axis_index("col")
    base = RIM

    def fetch(start):
        def go(lo, hi, kinds, part):
            for shard in range(devices):
                copy = pltpu.make_async_copy(
                    window.at[shard, lo:hi, 0:kinds],
                    blocks.at[base + lo : base + hi, 0:kinds, shard * quarter : (shard + 1) * quarter],
                    sem.at[part, shard],
                )
                copy.start() if start else copy.wait()

        go(RIM, RIM + rows, W, 0)

        @pl.when(r > 0)
        def _():
            go(0, RIM, W, 1)

        @pl.when(r < row_devices - 1)
        def _():
            go(RIM + rows, RIM + rows + 4, RIM, 2)
            go(RIM + rows + 4, span, 3, 3)

    blocks[0:RIM] = jnp.zeros((RIM,) + blocks.shape[1:], blocks.dtype)
    after = base + RIM + rows
    blocks[after : after + 4, RIM:W] = jnp.zeros((4, 1, B, B), blocks.dtype)
    blocks[after + 4 : after + RIM, 3:W] = jnp.zeros((3, W - 3, B, B), blocks.dtype)

    @pl.when(r == 0)
    def _():
        blocks[RIM : 2 * RIM] = jnp.zeros((RIM,) + blocks.shape[1:], blocks.dtype)

    @pl.when(r == row_devices - 1)
    def _():
        blocks[after : after + 4, 0:RIM] = jnp.zeros((4, RIM, B, B), blocks.dtype)
        blocks[after + 4 : after + RIM, 0:3] = jnp.zeros((3, 3, B, B), blocks.dtype)

    fetch(True)
    left[...] = jnp.zeros_like(left)
    filtered[...] = jnp.zeros_like(filtered)
    fetch(False)

    places = lax.broadcasted_iota(jnp.int32, (quarter, B), 0) + q * quarter
    select = (places == lax.broadcasted_iota(jnp.int32, (quarter, B), 1)).astype(jnp.bfloat16)
    own = pl.ds(pl.multiple_of(q * quarter, quarter), quarter)

    @pl.loop(0, rows)
    def _(i):
        strip = pl.ds(pl.multiple_of(i * quarter, quarter), quarter)
        at = base + RIM + i
        for d in range(W):
            left[at + d, strip, :] = blocks[at, d, own, :]
        for d in range(1, W):
            left[at - d, strip, :] = lax.dot_general(
                select, blocks[at - d, d], NT, preferred_element_type=jnp.float32
            ).astype(jnp.bfloat16)

    def column(lhs, c):
        at = base + c
        low_l = jnp.concatenate([lhs[at - d] for d in range(1, W)], axis=1)
        low_r = jnp.concatenate([blocks[at - d, d] for d in range(1, W)], axis=0)
        high_l = jnp.concatenate([lhs[at + d] for d in range(W)], axis=1)
        high_r = jnp.concatenate([blocks[at, d] for d in range(W)], axis=1)
        total = jnp.dot(low_l, low_r, preferred_element_type=jnp.float32)
        return total + lax.dot_general(
            high_l, high_r, NT, preferred_element_type=jnp.float32
        )

    @pl.loop(0, span)
    def _(c):
        square = column(left, c)
        for i in range(rows):
            piece = square[i * quarter : (i + 1) * quarter]
            kept = keep[i, c] != 0
            filtered[base + c, i * quarter : (i + 1) * quarter, :] = jnp.where(
                kept, piece, 0.0
            ).astype(jnp.bfloat16)
            offset = c - RIM - i

            @pl.when((offset >= 0) & (offset < W))
            def _(i=i, piece=piece, offset=offset):
                held[i, offset] = 3.0 * piece

    @pl.loop(RIM, span)
    def _(c):
        cube = column(filtered, c)
        for i in range(rows):
            piece = cube[i * quarter : (i + 1) * quarter]
            offset = c - RIM - i

            @pl.when((offset >= 0) & (offset < W))
            def _(i=i, piece=piece, offset=offset):
                held[i, offset] = held[i, offset] - 2.0 * piece

    first = r * rows
    for i in range(rows):
        for f in range(out.shape[1]):
            target = targets[first + i, f]
            there = target >= 0
            offset = jnp.where(there, target - first - i, 0)
            out[i, f] = jnp.where(there, held[i, offset], 0.0)


def per_device(row_devices, col_devices, upper_blocks, block_cols, filter_cols):
    rows, kinds, quarter, _ = upper_blocks.shape
    span = rows + 2 * RIM
    row_first = lax.axis_index("row") * rows

    own_ids = row_first + jnp.arange(rows, dtype=jnp.int32)
    span_ids = row_first - RIM + jnp.arange(span, dtype=jnp.int32)
    own_filter = lax.dynamic_slice_in_dim(filter_cols, row_first, rows, 0)
    padded_filter = jnp.pad(filter_cols, ((RIM, RIM), (0, 0)), constant_values=-1)
    span_filter = lax.dynamic_slice_in_dim(padded_filter, row_first, span, 0)
    upper = jnp.any(own_filter[:, None, :] == span_ids[None, :, None], axis=2)
    upper = upper & (span_ids >= 0)[None, :]
    lower = jnp.any(span_filter[None, :, :] == own_ids[:, None, None], axis=2)
    keep = (upper | lower).astype(jnp.int32)

    vmem = pl.BlockSpec(memory_space=pltpu.VMEM)
    smem = pl.BlockSpec(memory_space=pltpu.SMEM)
    anywhere = pl.BlockSpec(memory_space=pl.ANY)
    band = pl.pallas_call(
        band_kernel,
        out_shape=jax.ShapeDtypeStruct((rows, W, quarter, B), jnp.bfloat16),
        in_specs=[smem, vmem],
        out_specs=vmem,
        name="band_order",
    )(block_cols, upper_blocks)
    window = pl.pallas_call(
        functools.partial(gather_kernel, row_devices, col_devices),
        out_shape=jax.ShapeDtypeStruct((col_devices, span, W, quarter, B), jnp.bfloat16),
        in_specs=[anywhere],
        out_specs=anywhere,
        scratch_shapes=[
            pltpu.SemaphoreType.DMA,
            pltpu.SemaphoreType.DMA((2, col_devices)),
            pltpu.SemaphoreType.DMA((col_devices,)),
            pltpu.SemaphoreType.DMA((3, col_devices)),
            pltpu.SemaphoreType.DMA((3, col_devices)),
        ],
        compiler_params=pltpu.CompilerParams(collective_id=0, has_side_effects=True),
        name="gather_window",
    )(band)
    return pl.pallas_call(
        functools.partial(product_kernel, row_devices, rows, quarter),
        out_shape=jax.ShapeDtypeStruct((rows, filter_cols.shape[1], quarter, B), jnp.float32),
        in_specs=[smem, smem, anywhere],
        out_specs=vmem,
        scratch_shapes=[
            pltpu.VMEM((span + RIM, W, B, B), jnp.bfloat16),
            pltpu.VMEM((span + 2 * RIM, rows * quarter, B), jnp.bfloat16),
            pltpu.VMEM((span + 2 * RIM, rows * quarter, B), jnp.bfloat16),
            pltpu.VMEM((rows, W, quarter, B), jnp.float32),
            pltpu.SemaphoreType.DMA((4, col_devices)),
        ],
        compiler_params=pltpu.CompilerParams(vmem_limit_bytes=40 << 20),
        name="products",
    )(filter_cols, keep, window)


def solution(mesh):
    return jax.shard_map(
        functools.partial(per_device, mesh.shape["row"], mesh.shape["col"]),
        mesh=mesh,
        in_specs=(P("row", None, "col", None), P(), P()),
        out_specs=P("row", None, "col", None),
        check_vma=False,
    )
```

```python
import functools

import jax
import jax.numpy as jnp
from jax import lax
from jax.experimental import pallas as pl
from jax.experimental.pallas import tpu as pltpu
from jax.sharding import PartitionSpec as P

B = 128
W = 8
RIM = W - 1
MESH = pl.DeviceIdType.MESH
NT = (((1,), (1,)), ((), ()))


def row_chunks(rows):
    return [(lo, lo + 2) for lo in reversed(range(0, rows, 2))]


def band_kernel(cols, slots, out):
    rows, kinds = slots.shape[0], slots.shape[1]
    first = lax.axis_index("row") * rows
    out[...] = jnp.zeros_like(out)
    for i in range(rows):
        for k in range(kinds):
            column = cols[first + i, k]

            @pl.when(column >= 0)
            def _(i=i, k=k, column=column):
                out[i, column - first - i] = slots[i, k]


def gather_kernel(
    row_devices, col_devices, own, window, local_sem, col_send, col_recv, row_send, row_recv
):
    rows = own.shape[0]
    r, q = lax.axis_index("row"), lax.axis_index("col")
    has_next, has_before = r < row_devices - 1, r > 0
    has_up, has_down = q < col_devices - 1, q > 0
    next_row, before_row = {"row": r + 1}, {"row": r - 1}
    up_col, down_col = {"col": q + 1}, {"col": q - 1}
    neighbours = (
        (has_next, next_row), (has_before, before_row), (has_up, up_col), (has_down, down_col)
    )

    barrier = pltpu.get_barrier_semaphore()
    count = jnp.int32(0)
    for present, device in neighbours:

        @pl.when(present)
        def _(device=device):
            pl.semaphore_signal(barrier, inc=1, device_id=device, device_id_type=MESH)

        count = count + present.astype(jnp.int32)
    pl.semaphore_wait(barrier, count)

    local = pltpu.make_async_copy(own, window.at[q, RIM : RIM + rows], local_sem)
    local.start()
    chunks = row_chunks(rows)

    def source(shard, is_own, lo, hi):
        return own.at[lo:hi] if is_own else window.at[shard, RIM + lo : RIM + hi]

    def col_copy(shard, is_own, up, step, n):
        lo, hi = chunks[n]
        return pltpu.make_async_remote_copy(
            src_ref=source(shard, is_own, lo, hi),
            dst_ref=window.at[shard, RIM + lo : RIM + hi],
            send_sem=col_send.at[0 if up else 1, step, n],
            recv_sem=col_recv.at[shard, n],
            device_id=up_col if up else down_col,
            device_id_type=MESH,
        )

    def halo_copy(shard, is_own, onward, n):
        lo, hi = chunks[n]
        if onward:
            lo, kinds = max(lo, rows - RIM), W
            place, device = lo - (rows - RIM), next_row
        else:
            hi, kinds = min(hi, RIM), RIM - lo
            place, device = RIM + rows + lo, before_row
        return pltpu.make_async_remote_copy(
            src_ref=source(shard, is_own, lo, hi).at[:, 0:kinds],
            dst_ref=window.at[shard, place : place + hi - lo, 0:kinds],
            send_sem=row_send.at[0 if onward else 1, shard, n],
            recv_sem=row_recv.at[0 if onward else 1, shard, n],
            device_id=device,
            device_id_type=MESH,
        )

    def spread(shard, is_own, n):
        @pl.when(has_next)
        def _():
            halo_copy(shard, is_own, True, n).start()

        @pl.when(has_before)
        def _():
            halo_copy(shard, is_own, False, n).start()

    for n in range(len(chunks)):

        @pl.when(has_up)
        def _(n=n):
            col_copy(q, True, True, 0, n).start()

        @pl.when(has_down)
        def _(n=n):
            col_copy(q, True, False, 0, n).start()

        spread(q, True, n)

    for step in range(1, col_devices):
        for n in range(len(chunks)):
            for up in (True, False):
                shard = q - step if up else q + step
                arrives = shard >= 0 if up else shard < col_devices
                onward = has_up if up else has_down

                @pl.when(arrives)
                def _(shard=shard, up=up, onward=onward, step=step, n=n):
                    col_copy(shard, False, up, step, n).wait_recv()

                    @pl.when(onward)
                    def _():
                        col_copy(shard, False, up, step, n).start()

                    spread(shard, False, n)

    local.wait()
    for step in range(col_devices):
        for up in (True, False):
            shard = q - step if up else q + step
            arrives = shard >= 0 if up else shard < col_devices
            onward = has_up if up else has_down

            @pl.when(arrives & onward)
            def _(shard=shard, up=up, step=step):
                for n in range(len(chunks)):
                    col_copy(shard, step == 0, up, step, n).wait_send()

    for shard in range(col_devices):
        for present, onward in ((has_next, True), (has_before, False)):

            @pl.when(present)
            def _(shard=shard, onward=onward):
                for n in range(len(chunks)):
                    halo_copy(shard, False, onward, n).wait_send()
                    halo_copy(shard, False, not onward, n).wait_recv()


def product_kernel(
    row_devices, rows, quarter, targets, window, out, blocks, left, filtered, held, bits, sem
):
    span = rows + 2 * RIM
    devices = B // quarter
    r, q = lax.axis_index("row"), lax.axis_index("col")
    base = RIM
    later = [(lo, min(hi, RIM), RIM - lo) for lo, hi in row_chunks(rows) if lo < RIM]

    def fetch(start):
        def go(lo, hi, kinds, part):
            for shard in range(devices):
                copy = pltpu.make_async_copy(
                    window.at[shard, lo:hi, 0:kinds],
                    blocks.at[base + lo : base + hi, 0:kinds, shard * quarter : (shard + 1) * quarter],
                    sem.at[part, shard],
                )
                copy.start() if start else copy.wait()

        go(RIM, RIM + rows, W, 0)

        @pl.when(r > 0)
        def _():
            go(0, RIM, W, 1)

        @pl.when(r < row_devices - 1)
        def _():
            for n, (lo, hi, kinds) in enumerate(later):
                go(RIM + rows + lo, RIM + rows + hi, kinds, 2 + n)

    blocks[0:RIM] = jnp.zeros((RIM,) + blocks.shape[1:], blocks.dtype)
    after = base + RIM + rows
    for lo, hi, kinds in later:
        blocks[after + lo : after + hi, kinds:W] = jnp.zeros((hi - lo, W - kinds, B, B), blocks.dtype)

    @pl.when(r == 0)
    def _():
        blocks[RIM : 2 * RIM] = jnp.zeros((RIM,) + blocks.shape[1:], blocks.dtype)

    @pl.when(r == row_devices - 1)
    def _():
        for lo, hi, kinds in later:
            blocks[after + lo : after + hi, 0:kinds] = jnp.zeros((hi - lo, kinds, B, B), blocks.dtype)

    fetch(True)
    left[...] = jnp.zeros_like(left)
    filtered[...] = jnp.zeros_like(filtered)

    @pl.loop(0, span)
    def _(w):
        row = r * rows - RIM + w
        inside = (row >= 0) & (row < row_devices * rows)
        place = jnp.clip(row, 0, row_devices * rows - 1)
        word = jnp.int32(0)
        for f in range(out.shape[1]):
            target = targets[place, f]
            hit = inside & (target >= 0)
            word = word + jnp.where(hit, lax.shift_left(jnp.int32(1), jnp.where(hit, target - row, 0)), 0)
        bits[w] = word

    fetch(False)

    places = lax.broadcasted_iota(jnp.int32, (quarter, B), 0) + q * quarter
    select = (places == lax.broadcasted_iota(jnp.int32, (quarter, B), 1)).astype(jnp.bfloat16)
    own = pl.ds(pl.multiple_of(q * quarter, quarter), quarter)

    @pl.loop(0, rows)
    def _(i):
        strip = pl.ds(pl.multiple_of(i * quarter, quarter), quarter)
        at = base + RIM + i
        for d in range(W):
            left[at + d, strip, :] = blocks[at, d, own, :]
        for d in range(1, W):
            left[at - d, strip, :] = lax.dot_general(
                select, blocks[at - d, d], NT, preferred_element_type=jnp.float32
            ).astype(jnp.bfloat16)

    half = rows // 2
    full = (0, rows, W, W)
    early, late = (0, half, half, W), (half, rows, W, half)

    def column(lhs, c, shape):
        top, bottom, lows, highs = shape
        strip = slice(top * quarter, bottom * quarter)
        at = base + c
        low_l = jnp.concatenate([lhs[at - d, strip] for d in range(1, lows)], axis=1)
        low_r = jnp.concatenate([blocks[at - d, d] for d in range(1, lows)], axis=0)
        high_l = jnp.concatenate([lhs[at + d, strip] for d in range(highs)], axis=1)
        high_r = jnp.concatenate([blocks[at, d] for d in range(highs)], axis=1)
        total = jnp.dot(low_l, low_r, preferred_element_type=jnp.float32)
        total = total + lax.dot_general(
            high_l, high_r, NT, preferred_element_type=jnp.float32
        )
        return [
            (i, total[(i - top) * quarter : (i - top + 1) * quarter]) for i in range(top, bottom)
        ]

    def square_step(c, shape):
        for i, piece in column(left, c, shape):
            offset = c - RIM - i
            word = bits[jnp.minimum(c, RIM + i)]
            kept = (lax.shift_right_logical(word, jnp.abs(offset)) & 1) != 0
            filtered[base + c, i * quarter : (i + 1) * quarter, :] = jnp.where(
                kept, piece, 0.0
            ).astype(jnp.bfloat16)

            @pl.when((offset >= 0) & (offset < W))
            def _(i=i, piece=piece, offset=offset):
                held[i, offset] = 3.0 * piece

    def cube_step(c, shape):
        for i, piece in column(filtered, c, shape):
            offset = c - RIM - i

            @pl.when((offset >= 0) & (offset < W))
            def _(i=i, piece=piece, offset=offset):
                held[i, offset] = held[i, offset] - 2.0 * piece

    def sweep(lo, hi, body, shape):
        pl.loop(lo, hi)(lambda c: body(c, shape))

    sweep(0, half, square_step, early)
    sweep(half, span - half, square_step, full)
    sweep(span - half, span, square_step, late)
    sweep(RIM, RIM + half, cube_step, (0, half, W, W))
    sweep(RIM + half, span - half, cube_step, full)
    sweep(span - half, span, cube_step, late)

    first = r * rows
    for i in range(rows):
        for f in range(out.shape[1]):
            target = targets[first + i, f]
            there = target >= 0
            offset = jnp.where(there, target - first - i, 0)
            out[i, f] = jnp.where(there, held[i, offset], 0.0)


def per_device(row_devices, col_devices, upper_blocks, block_cols, filter_cols):
    rows, kinds, quarter, _ = upper_blocks.shape
    span = rows + 2 * RIM

    vmem = pl.BlockSpec(memory_space=pltpu.VMEM)
    smem = pl.BlockSpec(memory_space=pltpu.SMEM)
    anywhere = pl.BlockSpec(memory_space=pl.ANY)
    band = pl.pallas_call(
        band_kernel,
        out_shape=jax.ShapeDtypeStruct((rows, W, quarter, B), jnp.bfloat16),
        in_specs=[smem, vmem],
        out_specs=vmem,
        name="band_order",
    )(block_cols, upper_blocks)
    window = pl.pallas_call(
        functools.partial(gather_kernel, row_devices, col_devices),
        out_shape=jax.ShapeDtypeStruct((col_devices, span, W, quarter, B), jnp.bfloat16),
        in_specs=[anywhere],
        out_specs=anywhere,
        scratch_shapes=[
            pltpu.SemaphoreType.DMA,
            pltpu.SemaphoreType.DMA((2, col_devices, rows // 2)),
            pltpu.SemaphoreType.DMA((col_devices, rows // 2)),
            pltpu.SemaphoreType.DMA((2, col_devices, rows // 2)),
            pltpu.SemaphoreType.DMA((2, col_devices, rows // 2)),
        ],
        compiler_params=pltpu.CompilerParams(collective_id=0, has_side_effects=True),
        name="gather_window",
    )(band)
    return pl.pallas_call(
        functools.partial(product_kernel, row_devices, rows, quarter),
        out_shape=jax.ShapeDtypeStruct((rows, filter_cols.shape[1], quarter, B), jnp.float32),
        in_specs=[smem, anywhere],
        out_specs=vmem,
        scratch_shapes=[
            pltpu.VMEM((span + RIM, W, B, B), jnp.bfloat16),
            pltpu.VMEM((span + 2 * RIM, rows * quarter, B), jnp.bfloat16),
            pltpu.VMEM((span + 2 * RIM, rows * quarter, B), jnp.bfloat16),
            pltpu.VMEM((rows, W, quarter, B), jnp.float32),
            pltpu.SMEM((span,), jnp.int32),
            pltpu.SemaphoreType.DMA((2 + rows // 2, col_devices)),
        ],
        compiler_params=pltpu.CompilerParams(vmem_limit_bytes=40 << 20),
        name="products",
    )(filter_cols, window)


def solution(mesh):
    return jax.shard_map(
        functools.partial(per_device, mesh.shape["row"], mesh.shape["col"]),
        mesh=mesh,
        in_specs=(P("row", None, "col", None), P(), P()),
        out_specs=P("row", None, "col", None),
        check_vma=False,
    )
```

```python
import functools

import jax
import jax.numpy as jnp
from jax import lax
from jax.experimental import pallas as pl
from jax.experimental.pallas import tpu as pltpu
from jax.sharding import PartitionSpec as P

B = 128
W = 8
RIM = W - 1
MESH = pl.DeviceIdType.MESH
NT = (((1,), (1,)), ((), ()))


def row_chunks(rows):
    return [(lo, lo + 2) for lo in reversed(range(0, rows, 2))]


def gather_kernel(
    row_devices, col_devices, cols, slots, window,
    table, stored, own, local_sem, col_send, col_recv, row_send, row_recv
):
    rows, slot_count = slots.shape[0], slots.shape[1]
    r, q = lax.axis_index("row"), lax.axis_index("col")
    mine = pl.ds(pl.multiple_of(r * rows, rows), rows)
    table_copy = pltpu.make_async_copy(cols.at[mine], table, local_sem.at[0])
    slots_copy = pltpu.make_async_copy(slots, stored, local_sem.at[1])
    table_copy.start()
    slots_copy.start()
    has_next, has_before = r < row_devices - 1, r > 0
    has_up, has_down = q < col_devices - 1, q > 0
    next_row, before_row = {"row": r + 1}, {"row": r - 1}
    up_col, down_col = {"col": q + 1}, {"col": q - 1}
    neighbours = (
        (has_next, next_row), (has_before, before_row), (has_up, up_col), (has_down, down_col)
    )

    barrier = pltpu.get_barrier_semaphore()
    count = jnp.int32(0)
    for present, device in neighbours:

        @pl.when(present)
        def _(device=device):
            pl.semaphore_signal(barrier, inc=1, device_id=device, device_id_type=MESH)

        count = count + present.astype(jnp.int32)
    pl.semaphore_wait(barrier, count)

    local = pltpu.make_async_copy(own, window.at[q, RIM : RIM + rows], local_sem.at[2])
    chunks = row_chunks(rows)
    table_copy.wait()
    slots_copy.wait()
    first = r * rows

    def band_order(lo, hi):
        for i in range(lo, hi):
            offsets = [table[i, k] - first - i for k in range(slot_count)]
            for d in range(W):
                slot, found = jnp.int32(0), jnp.int32(0)
                for k in range(slot_count):
                    hit = offsets[k] == d
                    slot = jnp.where(hit, k, slot)
                    found = jnp.where(hit, 1, found)
                piece = stored[i, slot]
                own[i, d] = jnp.where(found > 0, piece, jnp.zeros_like(piece))

    def source(shard, is_own, lo, hi):
        return own.at[lo:hi] if is_own else window.at[shard, RIM + lo : RIM + hi]

    def col_copy(shard, is_own, up, step, n):
        lo, hi = chunks[n]
        return pltpu.make_async_remote_copy(
            src_ref=source(shard, is_own, lo, hi),
            dst_ref=window.at[shard, RIM + lo : RIM + hi],
            send_sem=col_send.at[0 if up else 1, step, n],
            recv_sem=col_recv.at[shard, n],
            device_id=up_col if up else down_col,
            device_id_type=MESH,
        )

    def halo_copy(shard, is_own, onward, n):
        lo, hi = chunks[n]
        if onward:
            lo, kinds = max(lo, rows - RIM), W
            place, device = lo - (rows - RIM), next_row
        else:
            hi, kinds = min(hi, RIM), RIM - lo
            place, device = RIM + rows + lo, before_row
        return pltpu.make_async_remote_copy(
            src_ref=source(shard, is_own, lo, hi).at[:, 0:kinds],
            dst_ref=window.at[shard, place : place + hi - lo, 0:kinds],
            send_sem=row_send.at[0 if onward else 1, shard, n],
            recv_sem=row_recv.at[0 if onward else 1, shard, n],
            device_id=device,
            device_id_type=MESH,
        )

    def spread(shard, is_own, n):
        @pl.when(has_next)
        def _():
            halo_copy(shard, is_own, True, n).start()

        @pl.when(has_before)
        def _():
            halo_copy(shard, is_own, False, n).start()

    for n in range(len(chunks)):
        band_order(*chunks[n])

        @pl.when(has_up)
        def _(n=n):
            col_copy(q, True, True, 0, n).start()

        @pl.when(has_down)
        def _(n=n):
            col_copy(q, True, False, 0, n).start()

        spread(q, True, n)

    local.start()

    for step in range(1, col_devices):
        for n in range(len(chunks)):
            for up in (True, False):
                shard = q - step if up else q + step
                arrives = shard >= 0 if up else shard < col_devices
                onward = has_up if up else has_down

                @pl.when(arrives)
                def _(shard=shard, up=up, onward=onward, step=step, n=n):
                    col_copy(shard, False, up, step, n).wait_recv()

                    @pl.when(onward)
                    def _():
                        col_copy(shard, False, up, step, n).start()

                    spread(shard, False, n)

    local.wait()
    for step in range(col_devices):
        for up in (True, False):
            shard = q - step if up else q + step
            arrives = shard >= 0 if up else shard < col_devices
            onward = has_up if up else has_down

            @pl.when(arrives & onward)
            def _(shard=shard, up=up, step=step):
                for n in range(len(chunks)):
                    col_copy(shard, step == 0, up, step, n).wait_send()

    for shard in range(col_devices):
        for present, onward in ((has_next, True), (has_before, False)):

            @pl.when(present)
            def _(shard=shard, onward=onward):
                for n in range(len(chunks)):
                    halo_copy(shard, False, onward, n).wait_send()
                    halo_copy(shard, False, not onward, n).wait_recv()


def product_kernel(
    row_devices, rows, quarter, filters, window, out, blocks, left, filtered, held, bits, targets, table_sem, sem
):
    span = rows + 2 * RIM
    devices = B // quarter
    r, q = lax.axis_index("row"), lax.axis_index("col")
    base = RIM
    later = [(lo, min(hi, RIM), RIM - lo) for lo, hi in row_chunks(rows) if lo < RIM]

    def fetch(start):
        def go(lo, hi, kinds, part):
            for shard in range(devices):
                copy = pltpu.make_async_copy(
                    window.at[shard, lo:hi, 0:kinds],
                    blocks.at[base + lo : base + hi, 0:kinds, shard * quarter : (shard + 1) * quarter],
                    sem.at[part, shard],
                )
                copy.start() if start else copy.wait()

        go(RIM, RIM + rows, W, 0)

        @pl.when(r > 0)
        def _():
            go(0, RIM, W, 1)

        @pl.when(r < row_devices - 1)
        def _():
            for n, (lo, hi, kinds) in enumerate(later):
                go(RIM + rows + lo, RIM + rows + hi, kinds, 2 + n)

    blocks[0:RIM] = jnp.zeros((RIM,) + blocks.shape[1:], blocks.dtype)
    after = base + RIM + rows
    for lo, hi, kinds in later:
        blocks[after + lo : after + hi, kinds:W] = jnp.zeros((hi - lo, W - kinds, B, B), blocks.dtype)

    @pl.when(r == 0)
    def _():
        blocks[RIM : 2 * RIM] = jnp.zeros((RIM,) + blocks.shape[1:], blocks.dtype)

    @pl.when(r == row_devices - 1)
    def _():
        for lo, hi, kinds in later:
            blocks[after + lo : after + hi, 0:kinds] = jnp.zeros((hi - lo, kinds, B, B), blocks.dtype)

    fetch(True)
    table_copy = pltpu.make_async_copy(filters, targets, table_sem)
    table_copy.start()
    left[...] = jnp.zeros_like(left)
    filtered[...] = jnp.zeros_like(filtered)
    table_copy.wait()

    @pl.loop(0, span)
    def _(w):
        row = r * rows - RIM + w
        inside = (row >= 0) & (row < row_devices * rows)
        place = jnp.clip(row, 0, row_devices * rows - 1)
        word = jnp.int32(0)
        for f in range(out.shape[1]):
            target = targets[place, f]
            hit = inside & (target >= 0)
            word = word + jnp.where(hit, lax.shift_left(jnp.int32(1), jnp.where(hit, target - row, 0)), 0)
        bits[w] = word

    fetch(False)

    places = lax.broadcasted_iota(jnp.int32, (quarter, B), 0) + q * quarter
    select = (places == lax.broadcasted_iota(jnp.int32, (quarter, B), 1)).astype(jnp.bfloat16)
    own = pl.ds(pl.multiple_of(q * quarter, quarter), quarter)

    @pl.loop(0, rows)
    def _(i):
        strip = pl.ds(pl.multiple_of(i * quarter, quarter), quarter)
        at = base + RIM + i
        for d in range(W):
            left[at + d, strip, :] = blocks[at, d, own, :]
        for d in range(1, W):
            left[at - d, strip, :] = lax.dot_general(
                select, blocks[at - d, d], NT, preferred_element_type=jnp.float32
            ).astype(jnp.bfloat16)

    half = rows // 2
    full = (0, rows, W, W)
    early, late = (0, half, half, W), (half, rows, W, half)

    def column(lhs, c, shape):
        top, bottom, lows, highs = shape
        strip = slice(top * quarter, bottom * quarter)
        at = base + c
        low_l = jnp.concatenate([lhs[at - d, strip] for d in range(1, lows)], axis=1)
        low_r = jnp.concatenate([blocks[at - d, d] for d in range(1, lows)], axis=0)
        high_l = jnp.concatenate([lhs[at + d, strip] for d in range(highs)], axis=1)
        high_r = jnp.concatenate([blocks[at, d] for d in range(highs)], axis=1)
        total = jnp.dot(low_l, low_r, preferred_element_type=jnp.float32)
        total = total + lax.dot_general(
            high_l, high_r, NT, preferred_element_type=jnp.float32
        )
        return [
            (i, total[(i - top) * quarter : (i - top + 1) * quarter]) for i in range(top, bottom)
        ]

    def square_step(c, shape):
        for i, piece in column(left, c, shape):
            offset = c - RIM - i
            word = bits[jnp.minimum(c, RIM + i)]
            kept = (lax.shift_right_logical(word, jnp.abs(offset)) & 1) != 0
            filtered[base + c, i * quarter : (i + 1) * quarter, :] = jnp.where(
                kept, piece, 0.0
            ).astype(jnp.bfloat16)

            @pl.when((offset >= 0) & (offset < W))
            def _(i=i, piece=piece, offset=offset):
                held[i, offset] = 3.0 * piece

    def cube_step(c, shape):
        for i, piece in column(filtered, c, shape):
            offset = c - RIM - i

            @pl.when((offset >= 0) & (offset < W))
            def _(i=i, piece=piece, offset=offset):
                held[i, offset] = held[i, offset] - 2.0 * piece

    def sweep(lo, hi, body, shape):
        pl.loop(lo, hi)(lambda c: body(c, shape))

    sweep(0, half, square_step, early)
    sweep(half, span - half, square_step, full)
    sweep(span - half, span, square_step, late)
    sweep(RIM, RIM + half, cube_step, (0, half, W, W))
    sweep(RIM + half, span - half, cube_step, full)
    sweep(span - half, span, cube_step, late)

    first = r * rows
    for i in range(rows):
        for f in range(out.shape[1]):
            target = targets[first + i, f]
            there = target >= 0
            offset = jnp.where(there, target - first - i, 0)
            out[i, f] = jnp.where(there, held[i, offset], 0.0)


def per_device(row_devices, col_devices, upper_blocks, block_cols, filter_cols):
    rows, kinds, quarter, _ = upper_blocks.shape
    span = rows + 2 * RIM

    vmem = pl.BlockSpec(memory_space=pltpu.VMEM)
    anywhere = pl.BlockSpec(memory_space=pl.ANY)
    window = pl.pallas_call(
        functools.partial(gather_kernel, row_devices, col_devices),
        out_shape=jax.ShapeDtypeStruct((col_devices, span, W, quarter, B), jnp.bfloat16),
        in_specs=[anywhere, anywhere],
        out_specs=anywhere,
        scratch_shapes=[
            pltpu.SMEM((rows, kinds), jnp.int32),
            pltpu.VMEM((rows, kinds, quarter, B), jnp.bfloat16),
            pltpu.VMEM((rows, W, quarter, B), jnp.bfloat16),
            pltpu.SemaphoreType.DMA((3,)),
            pltpu.SemaphoreType.DMA((2, col_devices, rows // 2)),
            pltpu.SemaphoreType.DMA((col_devices, rows // 2)),
            pltpu.SemaphoreType.DMA((2, col_devices, rows // 2)),
            pltpu.SemaphoreType.DMA((2, col_devices, rows // 2)),
        ],
        compiler_params=pltpu.CompilerParams(collective_id=0, has_side_effects=True),
        name="gather_window",
    )(block_cols, upper_blocks)
    return pl.pallas_call(
        functools.partial(product_kernel, row_devices, rows, quarter),
        out_shape=jax.ShapeDtypeStruct((rows, filter_cols.shape[1], quarter, B), jnp.float32),
        in_specs=[anywhere, anywhere],
        out_specs=vmem,
        scratch_shapes=[
            pltpu.VMEM((span + RIM, W, B, B), jnp.bfloat16),
            pltpu.VMEM((span + 2 * RIM, rows * quarter, B), jnp.bfloat16),
            pltpu.VMEM((span + 2 * RIM, rows * quarter, B), jnp.bfloat16),
            pltpu.VMEM((rows, W, quarter, B), jnp.float32),
            pltpu.SMEM((span,), jnp.int32),
            pltpu.SMEM(filter_cols.shape, jnp.int32),
            pltpu.SemaphoreType.DMA,
            pltpu.SemaphoreType.DMA((2 + rows // 2, col_devices)),
        ],
        compiler_params=pltpu.CompilerParams(vmem_limit_bytes=40 << 20),
        name="products",
    )(filter_cols, window)


def solution(mesh):
    return jax.shard_map(
        functools.partial(per_device, mesh.shape["row"], mesh.shape["col"]),
        mesh=mesh,
        in_specs=(P("row", None, "col", None), P(), P()),
        out_specs=P("row", None, "col", None),
        check_vma=False,
    )
```

```python
import functools

import jax
import jax.numpy as jnp
from jax import lax
from jax.experimental import pallas as pl
from jax.experimental.pallas import tpu as pltpu
from jax.sharding import PartitionSpec as P

B = 128
W = 8
RIM = W - 1
MESH = pl.DeviceIdType.MESH
NT = (((1,), (1,)), ((), ()))


def row_chunks(rows):
    return [(lo, lo + 2) for lo in reversed(range(0, rows, 2))]


def gather_kernel(
    row_devices, col_devices, cols, slots, window,
    table, stored, own, local_sem, col_send, col_recv, row_send, row_recv
):
    rows, slot_count = slots.shape[0], slots.shape[1]
    r, q = lax.axis_index("row"), lax.axis_index("col")
    table_copy = pltpu.make_async_copy(cols, table, local_sem.at[0])
    slots_copy = pltpu.make_async_copy(slots, stored, local_sem.at[1])
    table_copy.start()
    slots_copy.start()
    has_next, has_before = r < row_devices - 1, r > 0
    has_up, has_down = q < col_devices - 1, q > 0
    next_row, before_row = {"row": r + 1}, {"row": r - 1}
    up_col, down_col = {"col": q + 1}, {"col": q - 1}
    neighbours = (
        (has_next, next_row), (has_before, before_row), (has_up, up_col), (has_down, down_col)
    )

    barrier = pltpu.get_barrier_semaphore()
    count = jnp.int32(0)
    for present, device in neighbours:

        @pl.when(present)
        def _(device=device):
            pl.semaphore_signal(barrier, inc=1, device_id=device, device_id_type=MESH)

        count = count + present.astype(jnp.int32)
    pl.semaphore_wait(barrier, count)

    local = pltpu.make_async_copy(own, window.at[q, RIM : RIM + rows], local_sem.at[2])
    chunks = row_chunks(rows)
    table_copy.wait()
    slots_copy.wait()
    first = r * rows

    def band_order(lo, hi):
        for i in range(lo, hi):
            offsets = [table[k, first + i] - first - i for k in range(slot_count)]
            for d in range(W):
                slot, found = jnp.int32(0), jnp.int32(0)
                for k in range(slot_count):
                    hit = offsets[k] == d
                    slot = jnp.where(hit, k, slot)
                    found = jnp.where(hit, 1, found)
                piece = stored[i, slot]
                own[i, d] = jnp.where(found > 0, piece, jnp.zeros_like(piece))

    def source(shard, is_own, lo, hi):
        return own.at[lo:hi] if is_own else window.at[shard, RIM + lo : RIM + hi]

    def col_copy(shard, is_own, up, step, n):
        lo, hi = chunks[n]
        return pltpu.make_async_remote_copy(
            src_ref=source(shard, is_own, lo, hi),
            dst_ref=window.at[shard, RIM + lo : RIM + hi],
            send_sem=col_send.at[0 if up else 1, step, n],
            recv_sem=col_recv.at[shard, n],
            device_id=up_col if up else down_col,
            device_id_type=MESH,
        )

    def halo_copy(shard, is_own, onward, n):
        lo, hi = chunks[n]
        if onward:
            lo, kinds = max(lo, rows - RIM), W
            place, device = lo - (rows - RIM), next_row
        else:
            hi, kinds = min(hi, RIM), RIM - lo
            place, device = RIM + rows + lo, before_row
        return pltpu.make_async_remote_copy(
            src_ref=source(shard, is_own, lo, hi).at[:, 0:kinds],
            dst_ref=window.at[shard, place : place + hi - lo, 0:kinds],
            send_sem=row_send.at[0 if onward else 1, shard, n],
            recv_sem=row_recv.at[0 if onward else 1, shard, n],
            device_id=device,
            device_id_type=MESH,
        )

    def spread(shard, is_own, n):
        @pl.when(has_next)
        def _():
            halo_copy(shard, is_own, True, n).start()

        @pl.when(has_before)
        def _():
            halo_copy(shard, is_own, False, n).start()

    for n in range(len(chunks)):
        band_order(*chunks[n])

        @pl.when(has_up)
        def _(n=n):
            col_copy(q, True, True, 0, n).start()

        @pl.when(has_down)
        def _(n=n):
            col_copy(q, True, False, 0, n).start()

        spread(q, True, n)

    local.start()

    for step in range(1, col_devices):
        for n in range(len(chunks)):
            for up in (True, False):
                shard = q - step if up else q + step
                arrives = shard >= 0 if up else shard < col_devices
                onward = has_up if up else has_down

                @pl.when(arrives)
                def _(shard=shard, up=up, onward=onward, step=step, n=n):
                    col_copy(shard, False, up, step, n).wait_recv()

                    @pl.when(onward)
                    def _():
                        col_copy(shard, False, up, step, n).start()

                    spread(shard, False, n)

    local.wait()
    for step in range(col_devices):
        for up in (True, False):
            shard = q - step if up else q + step
            arrives = shard >= 0 if up else shard < col_devices
            onward = has_up if up else has_down

            @pl.when(arrives & onward)
            def _(shard=shard, up=up, step=step):
                for n in range(len(chunks)):
                    col_copy(shard, step == 0, up, step, n).wait_send()

    for shard in range(col_devices):
        for present, onward in ((has_next, True), (has_before, False)):

            @pl.when(present)
            def _(shard=shard, onward=onward):
                for n in range(len(chunks)):
                    halo_copy(shard, False, onward, n).wait_send()
                    halo_copy(shard, False, not onward, n).wait_recv()


def product_kernel(
    row_devices, rows, quarter, filters, window, out, blocks, left, filtered, held, bits, targets, table_sem, sem
):
    span = rows + 2 * RIM
    devices = B // quarter
    r, q = lax.axis_index("row"), lax.axis_index("col")
    base = RIM
    later = [(lo, min(hi, RIM), RIM - lo) for lo, hi in row_chunks(rows) if lo < RIM]

    def fetch(start):
        def go(lo, hi, kinds, part):
            for shard in range(devices):
                copy = pltpu.make_async_copy(
                    window.at[shard, lo:hi, 0:kinds],
                    blocks.at[base + lo : base + hi, 0:kinds, shard * quarter : (shard + 1) * quarter],
                    sem.at[part, shard],
                )
                copy.start() if start else copy.wait()

        go(RIM, RIM + rows, W, 0)

        @pl.when(r > 0)
        def _():
            go(0, RIM, W, 1)

        @pl.when(r < row_devices - 1)
        def _():
            for n, (lo, hi, kinds) in enumerate(later):
                go(RIM + rows + lo, RIM + rows + hi, kinds, 2 + n)

    blocks[0:RIM] = jnp.zeros((RIM,) + blocks.shape[1:], blocks.dtype)
    after = base + RIM + rows
    for lo, hi, kinds in later:
        blocks[after + lo : after + hi, kinds:W] = jnp.zeros((hi - lo, W - kinds, B, B), blocks.dtype)

    @pl.when(r == 0)
    def _():
        blocks[RIM : 2 * RIM] = jnp.zeros((RIM,) + blocks.shape[1:], blocks.dtype)

    @pl.when(r == row_devices - 1)
    def _():
        for lo, hi, kinds in later:
            blocks[after + lo : after + hi, 0:kinds] = jnp.zeros((hi - lo, kinds, B, B), blocks.dtype)

    fetch(True)
    table_copy = pltpu.make_async_copy(filters, targets, table_sem)
    table_copy.start()
    left[...] = jnp.zeros_like(left)
    filtered[...] = jnp.zeros_like(filtered)
    table_copy.wait()

    @pl.loop(0, span)
    def _(w):
        row = r * rows - RIM + w
        inside = (row >= 0) & (row < row_devices * rows)
        place = jnp.clip(row, 0, row_devices * rows - 1)
        word = jnp.int32(0)
        for f in range(out.shape[1]):
            target = targets[f, place]
            hit = inside & (target >= 0)
            word = word + jnp.where(hit, lax.shift_left(jnp.int32(1), jnp.where(hit, target - row, 0)), 0)
        bits[w] = word

    fetch(False)

    places = lax.broadcasted_iota(jnp.int32, (quarter, B), 0) + q * quarter
    select = (places == lax.broadcasted_iota(jnp.int32, (quarter, B), 1)).astype(jnp.bfloat16)
    own = pl.ds(pl.multiple_of(q * quarter, quarter), quarter)

    @pl.loop(0, rows)
    def _(i):
        strip = pl.ds(pl.multiple_of(i * quarter, quarter), quarter)
        at = base + RIM + i
        for d in range(W):
            left[at + d, strip, :] = blocks[at, d, own, :]
        for d in range(1, W):
            left[at - d, strip, :] = lax.dot_general(
                select, blocks[at - d, d], NT, preferred_element_type=jnp.float32
            ).astype(jnp.bfloat16)

    half = rows // 2
    full = (0, rows, W, W)
    early, late = (0, half, half, W), (half, rows, W, half)

    def column(lhs, c, shape):
        top, bottom, lows, highs = shape
        strip = slice(top * quarter, bottom * quarter)
        at = base + c
        low_l = jnp.concatenate([lhs[at - d, strip] for d in range(1, lows)], axis=1)
        low_r = jnp.concatenate([blocks[at - d, d] for d in range(1, lows)], axis=0)
        high_l = jnp.concatenate([lhs[at + d, strip] for d in range(highs)], axis=1)
        high_r = jnp.concatenate([blocks[at, d] for d in range(highs)], axis=1)
        total = jnp.dot(low_l, low_r, preferred_element_type=jnp.float32)
        total = total + lax.dot_general(
            high_l, high_r, NT, preferred_element_type=jnp.float32
        )
        return [
            (i, total[(i - top) * quarter : (i - top + 1) * quarter]) for i in range(top, bottom)
        ]

    def square_step(c, shape):
        for i, piece in column(left, c, shape):
            offset = c - RIM - i
            word = bits[jnp.minimum(c, RIM + i)]
            kept = (lax.shift_right_logical(word, jnp.abs(offset)) & 1) != 0
            filtered[base + c, i * quarter : (i + 1) * quarter, :] = jnp.where(
                kept, piece, 0.0
            ).astype(jnp.bfloat16)

            @pl.when((offset >= 0) & (offset < W))
            def _(i=i, piece=piece, offset=offset):
                held[i, offset] = 3.0 * piece

    def cube_step(c, shape):
        for i, piece in column(filtered, c, shape):
            offset = c - RIM - i

            @pl.when((offset >= 0) & (offset < W))
            def _(i=i, piece=piece, offset=offset):
                held[i, offset] = held[i, offset] - 2.0 * piece

    def sweep(lo, hi, body, shape):
        pl.loop(lo, hi)(lambda c: body(c, shape))

    sweep(0, half, square_step, early)
    sweep(half, span - half, square_step, full)
    sweep(span - half, span, square_step, late)
    sweep(RIM, RIM + half, cube_step, (0, half, W, W))
    sweep(RIM + half, span - half, cube_step, full)
    sweep(span - half, span, cube_step, late)

    first = r * rows
    for i in range(rows):
        for f in range(out.shape[1]):
            target = targets[f, first + i]
            there = target >= 0
            offset = jnp.where(there, target - first - i, 0)
            out[i, f] = jnp.where(there, held[i, offset], 0.0)


def per_device(row_devices, col_devices, upper_blocks, block_cols, filter_cols):
    rows, kinds, quarter, _ = upper_blocks.shape
    span = rows + 2 * RIM

    vmem = pl.BlockSpec(memory_space=pltpu.VMEM)
    anywhere = pl.BlockSpec(memory_space=pl.ANY)
    window = pl.pallas_call(
        functools.partial(gather_kernel, row_devices, col_devices),
        out_shape=jax.ShapeDtypeStruct((col_devices, span, W, quarter, B), jnp.bfloat16),
        in_specs=[anywhere, anywhere],
        out_specs=anywhere,
        scratch_shapes=[
            pltpu.SMEM((kinds, block_cols.shape[0]), jnp.int32),
            pltpu.VMEM((rows, kinds, quarter, B), jnp.bfloat16),
            pltpu.VMEM((rows, W, quarter, B), jnp.bfloat16),
            pltpu.SemaphoreType.DMA((3,)),
            pltpu.SemaphoreType.DMA((2, col_devices, rows // 2)),
            pltpu.SemaphoreType.DMA((col_devices, rows // 2)),
            pltpu.SemaphoreType.DMA((2, col_devices, rows // 2)),
            pltpu.SemaphoreType.DMA((2, col_devices, rows // 2)),
        ],
        compiler_params=pltpu.CompilerParams(collective_id=0, has_side_effects=True),
        name="gather_window",
    )(block_cols.T, upper_blocks)
    return pl.pallas_call(
        functools.partial(product_kernel, row_devices, rows, quarter),
        out_shape=jax.ShapeDtypeStruct((rows, filter_cols.shape[1], quarter, B), jnp.float32),
        in_specs=[anywhere, anywhere],
        out_specs=vmem,
        scratch_shapes=[
            pltpu.VMEM((span + RIM, W, B, B), jnp.bfloat16),
            pltpu.VMEM((span + 2 * RIM, rows * quarter, B), jnp.bfloat16),
            pltpu.VMEM((span + 2 * RIM, rows * quarter, B), jnp.bfloat16),
            pltpu.VMEM((rows, W, quarter, B), jnp.float32),
            pltpu.SMEM((span,), jnp.int32),
            pltpu.SMEM(filter_cols.shape[::-1], jnp.int32),
            pltpu.SemaphoreType.DMA,
            pltpu.SemaphoreType.DMA((2 + rows // 2, col_devices)),
        ],
        compiler_params=pltpu.CompilerParams(vmem_limit_bytes=60 << 20),
        name="products",
    )(filter_cols.T, window)


def solution(mesh):
    return jax.shard_map(
        functools.partial(per_device, mesh.shape["row"], mesh.shape["col"]),
        mesh=mesh,
        in_specs=(P("row", None, "col", None), P(), P()),
        out_specs=P("row", None, "col", None),
        check_vma=False,
    )
```

```python
import functools

import jax
import jax.numpy as jnp
from jax import lax
from jax.experimental import pallas as pl
from jax.experimental.pallas import tpu as pltpu
from jax.sharding import PartitionSpec as P

B = 128
W = 8
RIM = W - 1
MESH = pl.DeviceIdType.MESH
NT = (((1,), (1,)), ((), ()))


def row_chunks(rows):
    return [(lo, lo + 2) for lo in reversed(range(0, rows, 2))]


def gather_kernel(
    row_devices, col_devices, cols, slots, window,
    table, stored, own, local_sem, col_send, col_recv, row_send, row_recv
):
    rows, slot_count = slots.shape[0], slots.shape[1]
    r, q = lax.axis_index("row"), lax.axis_index("col")
    table_copy = pltpu.make_async_copy(cols, table, local_sem.at[0])
    slots_copy = pltpu.make_async_copy(slots, stored, local_sem.at[1])
    table_copy.start()
    slots_copy.start()
    has_next, has_before = r < row_devices - 1, r > 0
    has_up, has_down = q < col_devices - 1, q > 0
    next_row, before_row = {"row": r + 1}, {"row": r - 1}
    up_col, down_col = {"col": q + 1}, {"col": q - 1}
    neighbours = (
        (has_next, next_row), (has_before, before_row), (has_up, up_col), (has_down, down_col)
    )

    barrier = pltpu.get_barrier_semaphore()
    count = jnp.int32(0)
    for present, device in neighbours:

        @pl.when(present)
        def _(device=device):
            pl.semaphore_signal(barrier, inc=1, device_id=device, device_id_type=MESH)

        count = count + present.astype(jnp.int32)
    pl.semaphore_wait(barrier, count)

    local = pltpu.make_async_copy(own, window.at[q, RIM : RIM + rows], local_sem.at[2])
    chunks = row_chunks(rows)
    table_copy.wait()
    slots_copy.wait()
    first = r * rows

    def band_order(lo, hi):
        for i in range(lo, hi):
            offsets = [table[k, first + i] - first - i for k in range(slot_count)]
            for d in range(W):
                slot, found = jnp.int32(0), jnp.int32(0)
                for k in range(slot_count):
                    hit = offsets[k] == d
                    slot = jnp.where(hit, k, slot)
                    found = jnp.where(hit, 1, found)
                piece = stored[i, slot]
                own[i, d] = jnp.where(found > 0, piece, jnp.zeros_like(piece))

    def source(shard, is_own, lo, hi):
        return own.at[lo:hi] if is_own else window.at[shard, RIM + lo : RIM + hi]

    def col_copy(shard, is_own, up, step, n):
        lo, hi = chunks[n]
        return pltpu.make_async_remote_copy(
            src_ref=source(shard, is_own, lo, hi),
            dst_ref=window.at[shard, RIM + lo : RIM + hi],
            send_sem=col_send.at[0 if up else 1, step, n],
            recv_sem=col_recv.at[shard, n],
            device_id=up_col if up else down_col,
            device_id_type=MESH,
        )

    def halo_copy(shard, is_own, onward, n):
        lo, hi = chunks[n]
        if onward:
            lo, kinds = max(lo, rows - RIM), W
            place, device = lo - (rows - RIM), next_row
        else:
            hi, kinds = min(hi, RIM), RIM - lo
            place, device = RIM + rows + lo, before_row
        return pltpu.make_async_remote_copy(
            src_ref=source(shard, is_own, lo, hi).at[:, 0:kinds],
            dst_ref=window.at[shard, place : place + hi - lo, 0:kinds],
            send_sem=row_send.at[0 if onward else 1, shard, n],
            recv_sem=row_recv.at[0 if onward else 1, shard, n],
            device_id=device,
            device_id_type=MESH,
        )

    def spread(shard, is_own, n):
        @pl.when(has_next)
        def _():
            halo_copy(shard, is_own, True, n).start()

        @pl.when(has_before)
        def _():
            halo_copy(shard, is_own, False, n).start()

    for n in range(len(chunks)):
        band_order(*chunks[n])

        @pl.when(has_up)
        def _(n=n):
            col_copy(q, True, True, 0, n).start()

        @pl.when(has_down)
        def _(n=n):
            col_copy(q, True, False, 0, n).start()

        spread(q, True, n)

    local.start()

    for step in range(1, col_devices):
        for n in range(len(chunks)):
            for up in (True, False):
                shard = q - step if up else q + step
                arrives = shard >= 0 if up else shard < col_devices
                onward = has_up if up else has_down

                @pl.when(arrives)
                def _(shard=shard, up=up, onward=onward, step=step, n=n):
                    col_copy(shard, False, up, step, n).wait_recv()

                    @pl.when(onward)
                    def _():
                        col_copy(shard, False, up, step, n).start()

                    spread(shard, False, n)

    local.wait()
    for step in range(col_devices):
        for up in (True, False):
            shard = q - step if up else q + step
            arrives = shard >= 0 if up else shard < col_devices
            onward = has_up if up else has_down

            @pl.when(arrives & onward)
            def _(shard=shard, up=up, step=step):
                for n in range(len(chunks)):
                    col_copy(shard, step == 0, up, step, n).wait_send()

    for shard in range(col_devices):
        for present, onward in ((has_next, True), (has_before, False)):

            @pl.when(present)
            def _(shard=shard, onward=onward):
                for n in range(len(chunks)):
                    halo_copy(shard, False, onward, n).wait_send()
                    halo_copy(shard, False, not onward, n).wait_recv()


def product_kernel(
    row_devices, rows, quarter, filters, window, out, blocks, left, filtered, held, bits, targets, table_sem, sem
):
    span = rows + 2 * RIM
    devices = B // quarter
    r, q = lax.axis_index("row"), lax.axis_index("col")
    base = RIM
    later = [(lo, min(hi, RIM), RIM - lo) for lo, hi in row_chunks(rows) if lo < RIM]

    def fetch(start):
        def go(lo, hi, kinds, part):
            for shard in range(devices):
                copy = pltpu.make_async_copy(
                    window.at[shard, lo:hi, 0:kinds],
                    blocks.at[base + lo : base + hi, 0:kinds, shard * quarter : (shard + 1) * quarter],
                    sem.at[part, shard],
                )
                copy.start() if start else copy.wait()

        go(RIM, RIM + rows, W, 0)

        @pl.when(r > 0)
        def _():
            go(0, RIM, W, 1)

        @pl.when(r < row_devices - 1)
        def _():
            for n, (lo, hi, kinds) in enumerate(later):
                go(RIM + rows + lo, RIM + rows + hi, kinds, 2 + n)

    blocks[0:RIM] = jnp.zeros((RIM,) + blocks.shape[1:], blocks.dtype)
    after = base + RIM + rows
    for lo, hi, kinds in later:
        blocks[after + lo : after + hi, kinds:W] = jnp.zeros((hi - lo, W - kinds, B, B), blocks.dtype)

    @pl.when(r == 0)
    def _():
        blocks[RIM : 2 * RIM] = jnp.zeros((RIM,) + blocks.shape[1:], blocks.dtype)

    @pl.when(r == row_devices - 1)
    def _():
        for lo, hi, kinds in later:
            blocks[after + lo : after + hi, 0:kinds] = jnp.zeros((hi - lo, kinds, B, B), blocks.dtype)

    fetch(True)
    held[:, W] = jnp.zeros((rows, quarter, B), jnp.float32)
    table_copy = pltpu.make_async_copy(filters, targets, table_sem)
    table_copy.start()
    left[...] = jnp.zeros_like(left)
    filtered[...] = jnp.zeros_like(filtered)
    table_copy.wait()

    @pl.loop(0, span)
    def _(w):
        row = r * rows - RIM + w
        inside = (row >= 0) & (row < row_devices * rows)
        place = jnp.clip(row, 0, row_devices * rows - 1)
        word = jnp.int32(0)
        for f in range(out.shape[1]):
            target = targets[f, place]
            hit = inside & (target >= 0)
            word = word + jnp.where(hit, lax.shift_left(jnp.int32(1), jnp.where(hit, target - row, 0)), 0)
        bits[w] = word

    fetch(False)

    places = lax.broadcasted_iota(jnp.int32, (quarter, B), 0) + q * quarter
    select = (places == lax.broadcasted_iota(jnp.int32, (quarter, B), 1)).astype(jnp.bfloat16)
    own = pl.ds(pl.multiple_of(q * quarter, quarter), quarter)

    @pl.loop(0, rows)
    def _(i):
        strip = pl.ds(pl.multiple_of(i * quarter, quarter), quarter)
        at = base + RIM + i
        for d in range(W):
            left[at + d, strip, :] = blocks[at, d, own, :]
        for d in range(1, W):
            left[at - d, strip, :] = lax.dot_general(
                select, blocks[at - d, d], NT, preferred_element_type=jnp.float32
            ).astype(jnp.bfloat16)

    half = rows // 2
    full = (0, rows, W, W)
    early, late = (0, half, half, W), (half, rows, W, half)

    def column(lhs, c, shape):
        top, bottom, lows, highs = shape
        strip = slice(top * quarter, bottom * quarter)
        at = base + c
        low_l = jnp.concatenate([lhs[at - d, strip] for d in range(1, lows)], axis=1)
        low_r = jnp.concatenate([blocks[at - d, d] for d in range(1, lows)], axis=0)
        high_l = jnp.concatenate([lhs[at + d, strip] for d in range(highs)], axis=1)
        high_r = jnp.concatenate([blocks[at, d] for d in range(highs)], axis=1)
        total = jnp.dot(low_l, low_r, preferred_element_type=jnp.float32)
        total = total + lax.dot_general(
            high_l, high_r, NT, preferred_element_type=jnp.float32
        )
        return [
            (i, total[(i - top) * quarter : (i - top + 1) * quarter]) for i in range(top, bottom)
        ]

    def slot_of(offset):
        return jnp.where((offset >= 0) & (offset < W), offset, W)

    def square_step(c, pieces):
        for i, piece in pieces:
            offset = c - RIM - i
            word = bits[jnp.minimum(c, RIM + i)]
            kept = (lax.shift_right_logical(word, jnp.abs(offset)) & 1) != 0
            filtered[base + c, i * quarter : (i + 1) * quarter, :] = jnp.where(
                kept, piece, 0.0
            ).astype(jnp.bfloat16)
            held[i, slot_of(offset)] = 3.0 * piece

    def cube_step(c, pieces):
        for i, piece in pieces:
            offset = c - RIM - i
            held[i, slot_of(offset)] = held[i, slot_of(offset)] - 2.0 * piece

    def sweep(lo, hi, lhs, body, shape):
        pairs = (hi - lo) // 2

        @pl.loop(0, pairs)
        def _(n):
            c = lo + 2 * n
            one, two = column(lhs, c, shape), column(lhs, c + 1, shape)
            body(c, one)
            body(c + 1, two)

        if (hi - lo) % 2:
            body(jnp.int32(hi - 1), column(lhs, hi - 1, shape))

    sweep(0, half, left, square_step, early)
    sweep(half, span - half, left, square_step, full)
    sweep(span - half, span, left, square_step, late)
    sweep(RIM, RIM + half, filtered, cube_step, (0, half, W, W))
    sweep(RIM + half, span - half, filtered, cube_step, full)
    sweep(span - half, span, filtered, cube_step, late)

    first = r * rows
    for i in range(rows):
        for f in range(out.shape[1]):
            target = targets[f, first + i]
            there = target >= 0
            offset = jnp.where(there, target - first - i, 0)
            out[i, f] = jnp.where(there, held[i, offset], 0.0)


def per_device(row_devices, col_devices, upper_blocks, block_cols, filter_cols):
    rows, kinds, quarter, _ = upper_blocks.shape
    span = rows + 2 * RIM

    vmem = pl.BlockSpec(memory_space=pltpu.VMEM)
    anywhere = pl.BlockSpec(memory_space=pl.ANY)
    window = pl.pallas_call(
        functools.partial(gather_kernel, row_devices, col_devices),
        out_shape=jax.ShapeDtypeStruct((col_devices, span, W, quarter, B), jnp.bfloat16),
        in_specs=[anywhere, anywhere],
        out_specs=anywhere,
        scratch_shapes=[
            pltpu.SMEM((kinds, block_cols.shape[0]), jnp.int32),
            pltpu.VMEM((rows, kinds, quarter, B), jnp.bfloat16),
            pltpu.VMEM((rows, W, quarter, B), jnp.bfloat16),
            pltpu.SemaphoreType.DMA((3,)),
            pltpu.SemaphoreType.DMA((2, col_devices, rows // 2)),
            pltpu.SemaphoreType.DMA((col_devices, rows // 2)),
            pltpu.SemaphoreType.DMA((2, col_devices, rows // 2)),
            pltpu.SemaphoreType.DMA((2, col_devices, rows // 2)),
        ],
        compiler_params=pltpu.CompilerParams(collective_id=0, has_side_effects=True),
        name="gather_window",
    )(block_cols.T, upper_blocks)
    return pl.pallas_call(
        functools.partial(product_kernel, row_devices, rows, quarter),
        out_shape=jax.ShapeDtypeStruct((rows, filter_cols.shape[1], quarter, B), jnp.float32),
        in_specs=[anywhere, anywhere],
        out_specs=vmem,
        scratch_shapes=[
            pltpu.VMEM((span + RIM, W, B, B), jnp.bfloat16),
            pltpu.VMEM((span + 2 * RIM, rows * quarter, B), jnp.bfloat16),
            pltpu.VMEM((span + 2 * RIM, rows * quarter, B), jnp.bfloat16),
            pltpu.VMEM((rows, W + 1, quarter, B), jnp.float32),
            pltpu.SMEM((span,), jnp.int32),
            pltpu.SMEM(filter_cols.shape[::-1], jnp.int32),
            pltpu.SemaphoreType.DMA,
            pltpu.SemaphoreType.DMA((2 + rows // 2, col_devices)),
        ],
        compiler_params=pltpu.CompilerParams(vmem_limit_bytes=60 << 20),
        name="products",
    )(filter_cols.T, window)


def solution(mesh):
    return jax.shard_map(
        functools.partial(per_device, mesh.shape["row"], mesh.shape["col"]),
        mesh=mesh,
        in_specs=(P("row", None, "col", None), P(), P()),
        out_specs=P("row", None, "col", None),
        check_vma=False,
    )
```

```python
import functools

import jax
import jax.numpy as jnp
from jax import lax
from jax.experimental import pallas as pl
from jax.experimental.pallas import tpu as pltpu
from jax.sharding import PartitionSpec as P

B = 128
W = 8
RIM = W - 1
MESH = pl.DeviceIdType.MESH
NT = (((1,), (1,)), ((), ()))


def row_chunks(rows):
    return [(lo, lo + 1) for lo in reversed(range(rows))]


def gather_kernel(
    row_devices, col_devices, cols, slots, window,
    table, stored, own, local_sem, col_send, col_recv, row_send, row_recv
):
    rows, slot_count = slots.shape[0], slots.shape[1]
    r, q = lax.axis_index("row"), lax.axis_index("col")
    table_copy = pltpu.make_async_copy(cols, table, local_sem.at[0])
    slots_copy = pltpu.make_async_copy(slots, stored, local_sem.at[1])
    table_copy.start()
    slots_copy.start()
    has_next, has_before = r < row_devices - 1, r > 0
    has_up, has_down = q < col_devices - 1, q > 0
    next_row, before_row = {"row": r + 1}, {"row": r - 1}
    up_col, down_col = {"col": q + 1}, {"col": q - 1}
    neighbours = (
        (has_next, next_row), (has_before, before_row), (has_up, up_col), (has_down, down_col)
    )

    barrier = pltpu.get_barrier_semaphore()
    count = jnp.int32(0)
    for present, device in neighbours:

        @pl.when(present)
        def _(device=device):
            pl.semaphore_signal(barrier, inc=1, device_id=device, device_id_type=MESH)

        count = count + present.astype(jnp.int32)
    pl.semaphore_wait(barrier, count)

    local = pltpu.make_async_copy(own, window.at[q, RIM : RIM + rows], local_sem.at[2])
    chunks = row_chunks(rows)
    table_copy.wait()
    slots_copy.wait()
    first = r * rows

    def band_order(lo, hi):
        for i in range(lo, hi):
            offsets = [table[k, first + i] - first - i for k in range(slot_count)]
            for d in range(W):
                slot, found = jnp.int32(0), jnp.int32(0)
                for k in range(slot_count):
                    hit = offsets[k] == d
                    slot = jnp.where(hit, k, slot)
                    found = jnp.where(hit, 1, found)
                piece = stored[i, slot]
                own[i, d] = jnp.where(found > 0, piece, jnp.zeros_like(piece))

    def source(shard, is_own, lo, hi):
        return own.at[lo:hi] if is_own else window.at[shard, RIM + lo : RIM + hi]

    def col_copy(shard, is_own, up, step, n):
        lo, hi = chunks[n]
        return pltpu.make_async_remote_copy(
            src_ref=source(shard, is_own, lo, hi),
            dst_ref=window.at[shard, RIM + lo : RIM + hi],
            send_sem=col_send.at[0 if up else 1, step, n],
            recv_sem=col_recv.at[shard, n],
            device_id=up_col if up else down_col,
            device_id_type=MESH,
        )

    def has_halo(onward, n):
        return chunks[n][1] > rows - RIM if onward else chunks[n][0] < RIM

    def halo_copy(shard, is_own, onward, n):
        lo, hi = chunks[n]
        if onward:
            lo, kinds = max(lo, rows - RIM), W
            place, device = lo - (rows - RIM), next_row
        else:
            hi, kinds = min(hi, RIM), RIM - lo
            place, device = RIM + rows + lo, before_row
        return pltpu.make_async_remote_copy(
            src_ref=source(shard, is_own, lo, hi).at[:, 0:kinds],
            dst_ref=window.at[shard, place : place + hi - lo, 0:kinds],
            send_sem=row_send.at[0 if onward else 1, shard, n],
            recv_sem=row_recv.at[0 if onward else 1, shard, n],
            device_id=device,
            device_id_type=MESH,
        )

    def spread(shard, is_own, n):
        for present, onward in ((has_next, True), (has_before, False)):
            if has_halo(onward, n):

                @pl.when(present)
                def _(onward=onward):
                    halo_copy(shard, is_own, onward, n).start()

    for n in range(len(chunks)):
        band_order(*chunks[n])

        @pl.when(has_up)
        def _(n=n):
            col_copy(q, True, True, 0, n).start()

        @pl.when(has_down)
        def _(n=n):
            col_copy(q, True, False, 0, n).start()

        spread(q, True, n)

    local.start()

    for step in range(1, col_devices):
        for n in range(len(chunks)):
            for up in (True, False):
                shard = q - step if up else q + step
                arrives = shard >= 0 if up else shard < col_devices
                onward = has_up if up else has_down

                @pl.when(arrives)
                def _(shard=shard, up=up, onward=onward, step=step, n=n):
                    col_copy(shard, False, up, step, n).wait_recv()

                    @pl.when(onward)
                    def _():
                        col_copy(shard, False, up, step, n).start()

                    spread(shard, False, n)

    local.wait()
    for step in range(col_devices):
        for up in (True, False):
            shard = q - step if up else q + step
            arrives = shard >= 0 if up else shard < col_devices
            onward = has_up if up else has_down

            @pl.when(arrives & onward)
            def _(shard=shard, up=up, step=step):
                for n in range(len(chunks)):
                    col_copy(shard, step == 0, up, step, n).wait_send()

    for shard in range(col_devices):
        for present, onward in ((has_next, True), (has_before, False)):

            @pl.when(present)
            def _(shard=shard, onward=onward):
                for n in range(len(chunks)):
                    if has_halo(onward, n):
                        halo_copy(shard, False, onward, n).wait_send()
                    if has_halo(not onward, n):
                        halo_copy(shard, False, not onward, n).wait_recv()


def product_kernel(
    row_devices, rows, quarter, filters, window, out, blocks, left, filtered, held, bits, targets, table_sem, sem
):
    span = rows + 2 * RIM
    devices = B // quarter
    r, q = lax.axis_index("row"), lax.axis_index("col")
    base = RIM
    later = [(lo, min(hi, RIM), RIM - lo) for lo, hi in row_chunks(rows) if lo < RIM]

    def fetch(start):
        def go(lo, hi, kinds, part):
            for shard in range(devices):
                copy = pltpu.make_async_copy(
                    window.at[shard, lo:hi, 0:kinds],
                    blocks.at[base + lo : base + hi, 0:kinds, shard * quarter : (shard + 1) * quarter],
                    sem.at[part, shard],
                )
                copy.start() if start else copy.wait()

        go(RIM, RIM + rows, W, 0)

        @pl.when(r > 0)
        def _():
            go(0, RIM, W, 1)

        @pl.when(r < row_devices - 1)
        def _():
            for n, (lo, hi, kinds) in enumerate(later):
                go(RIM + rows + lo, RIM + rows + hi, kinds, 2 + n)

    blocks[0:RIM] = jnp.zeros((RIM,) + blocks.shape[1:], blocks.dtype)
    after = base + RIM + rows
    for lo, hi, kinds in later:
        blocks[after + lo : after + hi, kinds:W] = jnp.zeros((hi - lo, W - kinds, B, B), blocks.dtype)

    @pl.when(r == 0)
    def _():
        blocks[RIM : 2 * RIM] = jnp.zeros((RIM,) + blocks.shape[1:], blocks.dtype)

    @pl.when(r == row_devices - 1)
    def _():
        for lo, hi, kinds in later:
            blocks[after + lo : after + hi, 0:kinds] = jnp.zeros((hi - lo, kinds, B, B), blocks.dtype)

    fetch(True)
    held[:, W] = jnp.zeros((rows, quarter, B), jnp.float32)
    table_copy = pltpu.make_async_copy(filters, targets, table_sem)
    table_copy.start()
    left[...] = jnp.zeros_like(left)
    filtered[...] = jnp.zeros_like(filtered)
    table_copy.wait()

    @pl.loop(0, span)
    def _(w):
        row = r * rows - RIM + w
        inside = (row >= 0) & (row < row_devices * rows)
        place = jnp.clip(row, 0, row_devices * rows - 1)
        word = jnp.int32(0)
        for f in range(out.shape[1]):
            target = targets[f, place]
            hit = inside & (target >= 0)
            word = word + jnp.where(hit, lax.shift_left(jnp.int32(1), jnp.where(hit, target - row, 0)), 0)
        bits[w] = word

    fetch(False)

    places = lax.broadcasted_iota(jnp.int32, (quarter, B), 0) + q * quarter
    select = (places == lax.broadcasted_iota(jnp.int32, (quarter, B), 1)).astype(jnp.bfloat16)
    own = pl.ds(pl.multiple_of(q * quarter, quarter), quarter)

    def left_row(i):
        strip = pl.ds(pl.multiple_of(i * quarter, quarter), quarter)
        at = base + RIM + i
        for d in range(W):
            left[at + d, strip, :] = blocks[at, d, own, :]
        for d in range(1, W):
            left[at - d, strip, :] = lax.dot_general(
                select, blocks[at - d, d], NT, preferred_element_type=jnp.float32
            ).astype(jnp.bfloat16)

    @pl.loop(0, rows // 2)
    def _(n):
        left_row(2 * n)
        left_row(2 * n + 1)

    half = rows // 2
    full = (0, rows, W, W)
    early, late = (0, half, half, W), (half, rows, W, half)

    def column(lhs, c, shape):
        top, bottom, lows, highs = shape
        strip = slice(top * quarter, bottom * quarter)
        at = base + c
        low_l = jnp.concatenate([lhs[at - d, strip] for d in range(1, lows)], axis=1)
        low_r = jnp.concatenate([blocks[at - d, d] for d in range(1, lows)], axis=0)
        high_l = jnp.concatenate([lhs[at + d, strip] for d in range(highs)], axis=1)
        high_r = jnp.concatenate([blocks[at, d] for d in range(highs)], axis=1)
        total = jnp.dot(low_l, low_r, preferred_element_type=jnp.float32)
        total = total + lax.dot_general(
            high_l, high_r, NT, preferred_element_type=jnp.float32
        )
        return [
            (i, total[(i - top) * quarter : (i - top + 1) * quarter]) for i in range(top, bottom)
        ]

    def slot_of(offset):
        return jnp.where((offset >= 0) & (offset < W), offset, W)

    def square_step(c, pieces):
        for i, piece in pieces:
            offset = c - RIM - i
            word = bits[jnp.minimum(c, RIM + i)]
            kept = (lax.shift_right_logical(word, jnp.abs(offset)) & 1) != 0
            filtered[base + c, i * quarter : (i + 1) * quarter, :] = jnp.where(
                kept, piece, 0.0
            ).astype(jnp.bfloat16)
            held[i, slot_of(offset)] = 3.0 * piece

    def cube_step(c, pieces):
        for i, piece in pieces:
            offset = c - RIM - i
            held[i, slot_of(offset)] = held[i, slot_of(offset)] - 2.0 * piece

    def sweep(lo, hi, lhs, body, shape):
        pairs = (hi - lo) // 2

        @pl.loop(0, pairs)
        def _(n):
            c = lo + 2 * n
            one, two = column(lhs, c, shape), column(lhs, c + 1, shape)
            body(c, one)
            body(c + 1, two)

        if (hi - lo) % 2:
            body(jnp.int32(hi - 1), column(lhs, hi - 1, shape))

    sweep(0, half, left, square_step, early)
    sweep(half, span - half, left, square_step, full)
    sweep(span - half, span, left, square_step, late)
    sweep(RIM, RIM + half, filtered, cube_step, (0, half, W, W))
    sweep(RIM + half, span - half, filtered, cube_step, full)
    sweep(span - half, span, filtered, cube_step, late)

    first = r * rows
    for i in range(rows):
        for f in range(out.shape[1]):
            target = targets[f, first + i]
            there = target >= 0
            offset = jnp.where(there, target - first - i, 0)
            out[i, f] = jnp.where(there, held[i, offset], 0.0)


def per_device(row_devices, col_devices, upper_blocks, block_cols, filter_cols):
    rows, kinds, quarter, _ = upper_blocks.shape
    span = rows + 2 * RIM

    vmem = pl.BlockSpec(memory_space=pltpu.VMEM)
    anywhere = pl.BlockSpec(memory_space=pl.ANY)
    window = pl.pallas_call(
        functools.partial(gather_kernel, row_devices, col_devices),
        out_shape=jax.ShapeDtypeStruct((col_devices, span, W, quarter, B), jnp.bfloat16),
        in_specs=[anywhere, anywhere],
        out_specs=anywhere,
        scratch_shapes=[
            pltpu.SMEM((kinds, block_cols.shape[0]), jnp.int32),
            pltpu.VMEM((rows, kinds, quarter, B), jnp.bfloat16),
            pltpu.VMEM((rows, W, quarter, B), jnp.bfloat16),
            pltpu.SemaphoreType.DMA((3,)),
            pltpu.SemaphoreType.DMA((2, col_devices, rows)),
            pltpu.SemaphoreType.DMA((col_devices, rows)),
            pltpu.SemaphoreType.DMA((2, col_devices, rows)),
            pltpu.SemaphoreType.DMA((2, col_devices, rows)),
        ],
        compiler_params=pltpu.CompilerParams(collective_id=0, has_side_effects=True),
        name="gather_window",
    )(block_cols.T, upper_blocks)
    return pl.pallas_call(
        functools.partial(product_kernel, row_devices, rows, quarter),
        out_shape=jax.ShapeDtypeStruct((rows, filter_cols.shape[1], quarter, B), jnp.float32),
        in_specs=[anywhere, anywhere],
        out_specs=vmem,
        scratch_shapes=[
            pltpu.VMEM((span + RIM, W, B, B), jnp.bfloat16),
            pltpu.VMEM((span + 2 * RIM, rows * quarter, B), jnp.bfloat16),
            pltpu.VMEM((span + 2 * RIM, rows * quarter, B), jnp.bfloat16),
            pltpu.VMEM((rows, W + 1, quarter, B), jnp.float32),
            pltpu.SMEM((span,), jnp.int32),
            pltpu.SMEM(filter_cols.shape[::-1], jnp.int32),
            pltpu.SemaphoreType.DMA,
            pltpu.SemaphoreType.DMA((2 + rows, col_devices)),
        ],
        compiler_params=pltpu.CompilerParams(vmem_limit_bytes=60 << 20),
        name="products",
    )(filter_cols.T, window)


def solution(mesh):
    return jax.shard_map(
        functools.partial(per_device, mesh.shape["row"], mesh.shape["col"]),
        mesh=mesh,
        in_specs=(P("row", None, "col", None), P(), P()),
        out_specs=P("row", None, "col", None),
        check_vma=False,
    )
```

```python
import functools

import jax
import jax.numpy as jnp
from jax import lax
from jax.experimental import pallas as pl
from jax.experimental.pallas import tpu as pltpu
from jax.sharding import PartitionSpec as P

B = 128
W = 8
RIM = W - 1
MESH = pl.DeviceIdType.MESH
NT = (((1,), (1,)), ((), ()))


def row_chunks(rows):
    return [(lo, lo + 2) for lo in reversed(range(0, rows, 2))]


def gather_kernel(
    row_devices, col_devices, cols, slots, window,
    table, stored, own, local_sem, col_send, col_recv, row_send, row_recv
):
    rows, slot_count = slots.shape[0], slots.shape[1]
    r, q = lax.axis_index("row"), lax.axis_index("col")
    table_copy = pltpu.make_async_copy(cols, table, local_sem.at[0])
    slots_copy = pltpu.make_async_copy(slots, stored, local_sem.at[1])
    table_copy.start()
    slots_copy.start()
    has_next, has_before = r < row_devices - 1, r > 0
    has_up, has_down = q < col_devices - 1, q > 0
    next_row, before_row = {"row": r + 1}, {"row": r - 1}
    up_col, down_col = {"col": q + 1}, {"col": q - 1}
    neighbours = (
        (has_next, next_row), (has_before, before_row), (has_up, up_col), (has_down, down_col)
    )

    barrier = pltpu.get_barrier_semaphore()
    count = jnp.int32(0)
    for present, device in neighbours:

        @pl.when(present)
        def _(device=device):
            pl.semaphore_signal(barrier, inc=1, device_id=device, device_id_type=MESH)

        count = count + present.astype(jnp.int32)
    pl.semaphore_wait(barrier, count)

    local = pltpu.make_async_copy(own, window.at[q, RIM : RIM + rows], local_sem.at[2])
    chunks = row_chunks(rows)
    table_copy.wait()
    slots_copy.wait()
    first = r * rows

    def band_order(lo, hi):
        for i in range(lo, hi):
            offsets = [table[k, first + i] - first - i for k in range(slot_count)]
            for d in range(W):
                slot, found = jnp.int32(0), jnp.int32(0)
                for k in range(slot_count):
                    hit = offsets[k] == d
                    slot = jnp.where(hit, k, slot)
                    found = jnp.where(hit, 1, found)
                piece = stored[i, slot]
                own[i, d] = jnp.where(found > 0, piece, jnp.zeros_like(piece))

    def source(shard, is_own, lo, hi):
        return own.at[lo:hi] if is_own else window.at[shard, RIM + lo : RIM + hi]

    def col_copy(shard, is_own, up, step, n):
        lo, hi = chunks[n]
        return pltpu.make_async_remote_copy(
            src_ref=source(shard, is_own, lo, hi),
            dst_ref=window.at[shard, RIM + lo : RIM + hi],
            send_sem=col_send.at[0 if up else 1, step, n],
            recv_sem=col_recv.at[shard, n],
            device_id=up_col if up else down_col,
            device_id_type=MESH,
        )

    def has_halo(onward, n):
        return chunks[n][1] > rows - RIM if onward else chunks[n][0] < RIM

    def halo_copy(shard, is_own, onward, n):
        lo, hi = chunks[n]
        if onward:
            lo, kinds = max(lo, rows - RIM), W
            place, device = lo - (rows - RIM), next_row
        else:
            hi, kinds = min(hi, RIM), RIM - lo
            place, device = RIM + rows + lo, before_row
        return pltpu.make_async_remote_copy(
            src_ref=source(shard, is_own, lo, hi).at[:, 0:kinds],
            dst_ref=window.at[shard, place : place + hi - lo, 0:kinds],
            send_sem=row_send.at[0 if onward else 1, shard, n],
            recv_sem=row_recv.at[0 if onward else 1, shard, n],
            device_id=device,
            device_id_type=MESH,
        )

    def spread(shard, is_own, n):
        for present, onward in ((has_next, True), (has_before, False)):
            if has_halo(onward, n):

                @pl.when(present)
                def _(onward=onward):
                    halo_copy(shard, is_own, onward, n).start()

    for n in range(len(chunks)):
        band_order(*chunks[n])

        @pl.when(has_up)
        def _(n=n):
            col_copy(q, True, True, 0, n).start()

        @pl.when(has_down)
        def _(n=n):
            col_copy(q, True, False, 0, n).start()

    for n in range(len(chunks)):
        spread(q, True, n)

    local.start()

    for step in range(1, col_devices):
        for n in range(len(chunks)):
            for up in (True, False):
                shard = q - step if up else q + step
                arrives = shard >= 0 if up else shard < col_devices
                onward = has_up if up else has_down

                @pl.when(arrives)
                def _(shard=shard, up=up, onward=onward, step=step, n=n):
                    col_copy(shard, False, up, step, n).wait_recv()

                    @pl.when(onward)
                    def _():
                        col_copy(shard, False, up, step, n).start()

                    spread(shard, False, n)

    local.wait()
    for step in range(col_devices):
        for up in (True, False):
            shard = q - step if up else q + step
            arrives = shard >= 0 if up else shard < col_devices
            onward = has_up if up else has_down

            @pl.when(arrives & onward)
            def _(shard=shard, up=up, step=step):
                for n in range(len(chunks)):
                    col_copy(shard, step == 0, up, step, n).wait_send()

    for shard in range(col_devices):
        for present, onward in ((has_next, True), (has_before, False)):

            @pl.when(present)
            def _(shard=shard, onward=onward):
                for n in range(len(chunks)):
                    if has_halo(onward, n):
                        halo_copy(shard, False, onward, n).wait_send()
                    if has_halo(not onward, n):
                        halo_copy(shard, False, not onward, n).wait_recv()


def product_kernel(
    row_devices, rows, quarter, filters, window, out, blocks, left, filtered, held, bits, targets, table_sem, sem
):
    span = rows + 2 * RIM
    devices = B // quarter
    r, q = lax.axis_index("row"), lax.axis_index("col")
    base = RIM
    later = [(lo, min(hi, RIM), RIM - lo) for lo, hi in row_chunks(rows) if lo < RIM]

    def fetch(start):
        def go(lo, hi, kinds, part):
            for shard in range(devices):
                copy = pltpu.make_async_copy(
                    window.at[shard, lo:hi, 0:kinds],
                    blocks.at[base + lo : base + hi, 0:kinds, shard * quarter : (shard + 1) * quarter],
                    sem.at[part, shard],
                )
                copy.start() if start else copy.wait()

        go(RIM, RIM + rows, W, 0)

        @pl.when(r > 0)
        def _():
            go(0, RIM, W, 1)

        @pl.when(r < row_devices - 1)
        def _():
            for n, (lo, hi, kinds) in enumerate(later):
                go(RIM + rows + lo, RIM + rows + hi, kinds, 2 + n)

    blocks[0:RIM] = jnp.zeros((RIM,) + blocks.shape[1:], blocks.dtype)
    after = base + RIM + rows
    for lo, hi, kinds in later:
        blocks[after + lo : after + hi, kinds:W] = jnp.zeros((hi - lo, W - kinds, B, B), blocks.dtype)

    @pl.when(r == 0)
    def _():
        blocks[RIM : 2 * RIM] = jnp.zeros((RIM,) + blocks.shape[1:], blocks.dtype)

    @pl.when(r == row_devices - 1)
    def _():
        for lo, hi, kinds in later:
            blocks[after + lo : after + hi, 0:kinds] = jnp.zeros((hi - lo, kinds, B, B), blocks.dtype)

    fetch(True)
    held[:, W] = jnp.zeros((rows, quarter, B), jnp.float32)
    table_copy = pltpu.make_async_copy(filters, targets, table_sem)
    table_copy.start()
    left[...] = jnp.zeros_like(left)
    filtered[...] = jnp.zeros_like(filtered)
    table_copy.wait()

    @pl.loop(0, span)
    def _(w):
        row = r * rows - RIM + w
        inside = (row >= 0) & (row < row_devices * rows)
        place = jnp.clip(row, 0, row_devices * rows - 1)
        word = jnp.int32(0)
        for f in range(out.shape[1]):
            target = targets[f, place]
            hit = inside & (target >= 0)
            word = word + jnp.where(hit, lax.shift_left(jnp.int32(1), jnp.where(hit, target - row, 0)), 0)
        bits[w] = word

    fetch(False)

    places = lax.broadcasted_iota(jnp.int32, (quarter, B), 0) + q * quarter
    select = (places == lax.broadcasted_iota(jnp.int32, (quarter, B), 1)).astype(jnp.bfloat16)
    own = pl.ds(pl.multiple_of(q * quarter, quarter), quarter)

    def left_row(i):
        strip = pl.ds(pl.multiple_of(i * quarter, quarter), quarter)
        at = base + RIM + i
        for d in range(W):
            left[at + d, strip, :] = blocks[at, d, own, :]
        for d in range(1, W):
            left[at - d, strip, :] = lax.dot_general(
                select, blocks[at - d, d], NT, preferred_element_type=jnp.float32
            ).astype(jnp.bfloat16)

    @pl.loop(0, rows // 2)
    def _(n):
        left_row(2 * n)
        left_row(2 * n + 1)

    half = rows // 2
    full = (0, rows, W, W)
    early, late = (0, half, half, W), (half, rows, W, half)

    def column(lhs, c, shape):
        top, bottom, lows, highs = shape
        strip = slice(top * quarter, bottom * quarter)
        at = base + c
        low_l = jnp.concatenate([lhs[at - d, strip] for d in range(1, lows)], axis=1)
        low_r = jnp.concatenate([blocks[at - d, d] for d in range(1, lows)], axis=0)
        high_l = jnp.concatenate([lhs[at + d, strip] for d in range(highs)], axis=1)
        high_r = jnp.concatenate([blocks[at, d] for d in range(highs)], axis=1)
        total = jnp.dot(low_l, low_r, preferred_element_type=jnp.float32)
        total = total + lax.dot_general(
            high_l, high_r, NT, preferred_element_type=jnp.float32
        )
        return [
            (i, total[(i - top) * quarter : (i - top + 1) * quarter]) for i in range(top, bottom)
        ]

    def slot_of(offset):
        return jnp.where((offset >= 0) & (offset < W), offset, W)

    def square_step(c, pieces):
        for i, piece in pieces:
            offset = c - RIM - i
            word = bits[jnp.minimum(c, RIM + i)]
            kept = (lax.shift_right_logical(word, jnp.abs(offset)) & 1) != 0
            filtered[base + c, i * quarter : (i + 1) * quarter, :] = jnp.where(
                kept, piece, 0.0
            ).astype(jnp.bfloat16)
            held[i, slot_of(offset)] = 3.0 * piece

    def cube_step(c, pieces):
        for i, piece in pieces:
            offset = c - RIM - i
            held[i, slot_of(offset)] = held[i, slot_of(offset)] - 2.0 * piece

    def sweep(lo, hi, lhs, body, shape):
        pairs = (hi - lo) // 2

        @pl.loop(0, pairs)
        def _(n):
            c = lo + 2 * n
            one, two = column(lhs, c, shape), column(lhs, c + 1, shape)
            body(c, one)
            body(c + 1, two)

        if (hi - lo) % 2:
            body(jnp.int32(hi - 1), column(lhs, hi - 1, shape))

    sweep(0, half, left, square_step, early)
    sweep(half, span - half, left, square_step, full)
    sweep(span - half, span, left, square_step, late)
    sweep(RIM, RIM + half, filtered, cube_step, (0, half, W, W))
    sweep(RIM + half, span - half, filtered, cube_step, full)
    sweep(span - half, span, filtered, cube_step, late)

    first = r * rows
    for i in range(rows):
        for f in range(out.shape[1]):
            target = targets[f, first + i]
            there = target >= 0
            offset = jnp.where(there, target - first - i, 0)
            out[i, f] = jnp.where(there, held[i, offset], 0.0)


def per_device(row_devices, col_devices, upper_blocks, block_cols, filter_cols):
    rows, kinds, quarter, _ = upper_blocks.shape
    span = rows + 2 * RIM

    vmem = pl.BlockSpec(memory_space=pltpu.VMEM)
    anywhere = pl.BlockSpec(memory_space=pl.ANY)
    window = pl.pallas_call(
        functools.partial(gather_kernel, row_devices, col_devices),
        out_shape=jax.ShapeDtypeStruct((col_devices, span, W, quarter, B), jnp.bfloat16),
        in_specs=[anywhere, anywhere],
        out_specs=anywhere,
        scratch_shapes=[
            pltpu.SMEM((kinds, block_cols.shape[0]), jnp.int32),
            pltpu.VMEM((rows, kinds, quarter, B), jnp.bfloat16),
            pltpu.VMEM((rows, W, quarter, B), jnp.bfloat16),
            pltpu.SemaphoreType.DMA((3,)),
            pltpu.SemaphoreType.DMA((2, col_devices, rows)),
            pltpu.SemaphoreType.DMA((col_devices, rows)),
            pltpu.SemaphoreType.DMA((2, col_devices, rows)),
            pltpu.SemaphoreType.DMA((2, col_devices, rows)),
        ],
        compiler_params=pltpu.CompilerParams(collective_id=0, has_side_effects=True),
        name="gather_window",
    )(block_cols.T, upper_blocks)
    return pl.pallas_call(
        functools.partial(product_kernel, row_devices, rows, quarter),
        out_shape=jax.ShapeDtypeStruct((rows, filter_cols.shape[1], quarter, B), jnp.float32),
        in_specs=[anywhere, anywhere],
        out_specs=vmem,
        scratch_shapes=[
            pltpu.VMEM((span + RIM, W, B, B), jnp.bfloat16),
            pltpu.VMEM((span + 2 * RIM, rows * quarter, B), jnp.bfloat16),
            pltpu.VMEM((span + 2 * RIM, rows * quarter, B), jnp.bfloat16),
            pltpu.VMEM((rows, W + 1, quarter, B), jnp.float32),
            pltpu.SMEM((span,), jnp.int32),
            pltpu.SMEM(filter_cols.shape[::-1], jnp.int32),
            pltpu.SemaphoreType.DMA,
            pltpu.SemaphoreType.DMA((2 + rows, col_devices)),
        ],
        compiler_params=pltpu.CompilerParams(vmem_limit_bytes=60 << 20),
        name="products",
    )(filter_cols.T, window)


def solution(mesh):
    return jax.shard_map(
        functools.partial(per_device, mesh.shape["row"], mesh.shape["col"]),
        mesh=mesh,
        in_specs=(P("row", None, "col", None), P(), P()),
        out_specs=P("row", None, "col", None),
        check_vma=False,
    )
```

```python
import functools

import jax
import jax.numpy as jnp
from jax import lax
from jax.experimental import pallas as pl
from jax.experimental.pallas import tpu as pltpu
from jax.sharding import PartitionSpec as P

B = 128
W = 8
RIM = W - 1
MESH = pl.DeviceIdType.MESH
NT = (((1,), (1,)), ((), ()))


def row_chunks(rows):
    return [(lo, lo + 2) for lo in reversed(range(0, rows, 2))]


def gather_kernel(
    row_devices, col_devices, cols, slots, window,
    table, stored, own, local_sem, col_send, col_recv, row_send, row_recv
):
    rows, slot_count = slots.shape[0], slots.shape[1]
    r, q = lax.axis_index("row"), lax.axis_index("col")
    table_copy = pltpu.make_async_copy(cols, table, local_sem.at[0])
    slots_copy = pltpu.make_async_copy(slots, stored, local_sem.at[1])
    table_copy.start()
    slots_copy.start()
    has_next, has_before = r < row_devices - 1, r > 0
    has_up, has_down = q < col_devices - 1, q > 0
    next_row, before_row = {"row": r + 1}, {"row": r - 1}
    up_col, down_col = {"col": q + 1}, {"col": q - 1}
    neighbours = (
        (has_next, next_row), (has_before, before_row), (has_up, up_col), (has_down, down_col)
    )

    barrier = pltpu.get_barrier_semaphore()
    count = jnp.int32(0)
    for present, device in neighbours:

        @pl.when(present)
        def _(device=device):
            pl.semaphore_signal(barrier, inc=1, device_id=device, device_id_type=MESH)

        count = count + present.astype(jnp.int32)
    pl.semaphore_wait(barrier, count)

    local = pltpu.make_async_copy(own, window.at[q, RIM : RIM + rows], local_sem.at[2])
    chunks = row_chunks(rows)
    table_copy.wait()
    slots_copy.wait()
    first = r * rows

    def band_order(lo, hi):
        for i in range(lo, hi):
            offsets = [table[k, first + i] - first - i for k in range(slot_count)]
            for d in range(W):
                slot, found = jnp.int32(0), jnp.int32(0)
                for k in range(slot_count):
                    hit = offsets[k] == d
                    slot = jnp.where(hit, k, slot)
                    found = jnp.where(hit, 1, found)
                piece = stored[i, slot]
                own[i, d] = jnp.where(found > 0, piece, jnp.zeros_like(piece))

    def source(shard, is_own, lo, hi):
        return own.at[lo:hi] if is_own else window.at[shard, RIM + lo : RIM + hi]

    def col_copy(shard, is_own, up, step, n):
        lo, hi = chunks[n]
        return pltpu.make_async_remote_copy(
            src_ref=source(shard, is_own, lo, hi),
            dst_ref=window.at[shard, RIM + lo : RIM + hi],
            send_sem=col_send.at[0 if up else 1, step, n],
            recv_sem=col_recv.at[shard, n],
            device_id=up_col if up else down_col,
            device_id_type=MESH,
        )

    def has_halo(onward, n):
        return chunks[n][1] > rows - RIM if onward else chunks[n][0] < RIM

    def halo_copy(shard, is_own, onward, n):
        lo, hi = chunks[n]
        if onward:
            lo, kinds = max(lo, rows - RIM), W
            place, device = lo - (rows - RIM), next_row
        else:
            hi, kinds = min(hi, RIM), RIM - lo
            place, device = RIM + rows + lo, before_row
        return pltpu.make_async_remote_copy(
            src_ref=source(shard, is_own, lo, hi).at[:, 0:kinds],
            dst_ref=window.at[shard, place : place + hi - lo, 0:kinds],
            send_sem=row_send.at[0 if onward else 1, shard, n],
            recv_sem=row_recv.at[0 if onward else 1, shard, n],
            device_id=device,
            device_id_type=MESH,
        )

    def spread(shard, is_own, n):
        for present, onward in ((has_next, True), (has_before, False)):
            if has_halo(onward, n):

                @pl.when(present)
                def _(onward=onward):
                    halo_copy(shard, is_own, onward, n).start()

    for n in range(len(chunks)):
        band_order(*chunks[n])
        spread(q, True, n)

        @pl.when(has_up)
        def _(n=n):
            col_copy(q, True, True, 0, n).start()

        @pl.when(has_down)
        def _(n=n):
            col_copy(q, True, False, 0, n).start()

    local.start()

    for step in range(1, col_devices):
        for n in range(len(chunks)):
            for up in (True, False):
                shard = q - step if up else q + step
                arrives = shard >= 0 if up else shard < col_devices
                onward = has_up if up else has_down

                @pl.when(arrives)
                def _(shard=shard, up=up, onward=onward, step=step, n=n):
                    col_copy(shard, False, up, step, n).wait_recv()
                    spread(shard, False, n)

                    @pl.when(onward)
                    def _():
                        col_copy(shard, False, up, step, n).start()

    local.wait()
    for step in range(col_devices):
        for up in (True, False):
            shard = q - step if up else q + step
            arrives = shard >= 0 if up else shard < col_devices
            onward = has_up if up else has_down

            @pl.when(arrives & onward)
            def _(shard=shard, up=up, step=step):
                for n in range(len(chunks)):
                    col_copy(shard, step == 0, up, step, n).wait_send()

    for shard in range(col_devices):
        for present, onward in ((has_next, True), (has_before, False)):

            @pl.when(present)
            def _(shard=shard, onward=onward):
                for n in range(len(chunks)):
                    if has_halo(onward, n):
                        halo_copy(shard, False, onward, n).wait_send()
                    if has_halo(not onward, n):
                        halo_copy(shard, False, not onward, n).wait_recv()


def product_kernel(
    row_devices, rows, quarter, filters, window, out, blocks, left, filtered, held, bits, targets, table_sem, sem
):
    span = rows + 2 * RIM
    devices = B // quarter
    r, q = lax.axis_index("row"), lax.axis_index("col")
    base = RIM
    later = [(lo, min(hi, RIM), RIM - lo) for lo, hi in row_chunks(rows) if lo < RIM]

    def fetch(start):
        def go(lo, hi, kinds, part):
            for shard in range(devices):
                copy = pltpu.make_async_copy(
                    window.at[shard, lo:hi, 0:kinds],
                    blocks.at[base + lo : base + hi, 0:kinds, shard * quarter : (shard + 1) * quarter],
                    sem.at[part, shard],
                )
                copy.start() if start else copy.wait()

        go(RIM, RIM + rows, W, 0)

        @pl.when(r > 0)
        def _():
            go(0, RIM, W, 1)

        @pl.when(r < row_devices - 1)
        def _():
            for n, (lo, hi, kinds) in enumerate(later):
                go(RIM + rows + lo, RIM + rows + hi, kinds, 2 + n)

    blocks[0:RIM] = jnp.zeros((RIM,) + blocks.shape[1:], blocks.dtype)
    after = base + RIM + rows
    for lo, hi, kinds in later:
        blocks[after + lo : after + hi, kinds:W] = jnp.zeros((hi - lo, W - kinds, B, B), blocks.dtype)

    @pl.when(r == 0)
    def _():
        blocks[RIM : 2 * RIM] = jnp.zeros((RIM,) + blocks.shape[1:], blocks.dtype)

    @pl.when(r == row_devices - 1)
    def _():
        for lo, hi, kinds in later:
            blocks[after + lo : after + hi, 0:kinds] = jnp.zeros((hi - lo, kinds, B, B), blocks.dtype)

    fetch(True)
    held[:, W] = jnp.zeros((rows, quarter, B), jnp.float32)
    table_copy = pltpu.make_async_copy(filters, targets, table_sem)
    table_copy.start()
    left[...] = jnp.zeros_like(left)
    filtered[...] = jnp.zeros_like(filtered)
    table_copy.wait()

    @pl.loop(0, span)
    def _(w):
        row = r * rows - RIM + w
        inside = (row >= 0) & (row < row_devices * rows)
        place = jnp.clip(row, 0, row_devices * rows - 1)
        word = jnp.int32(0)
        for f in range(out.shape[1]):
            target = targets[f, place]
            hit = inside & (target >= 0)
            word = word + jnp.where(hit, lax.shift_left(jnp.int32(1), jnp.where(hit, target - row, 0)), 0)
        bits[w] = word

    fetch(False)

    places = lax.broadcasted_iota(jnp.int32, (quarter, B), 0) + q * quarter
    select = (places == lax.broadcasted_iota(jnp.int32, (quarter, B), 1)).astype(jnp.bfloat16)
    own = pl.ds(pl.multiple_of(q * quarter, quarter), quarter)

    def left_row(i):
        strip = pl.ds(pl.multiple_of(i * quarter, quarter), quarter)
        at = base + RIM + i
        for d in range(W):
            left[at + d, strip, :] = blocks[at, d, own, :]
        for d in range(1, W):
            left[at - d, strip, :] = lax.dot_general(
                select, blocks[at - d, d], NT, preferred_element_type=jnp.float32
            ).astype(jnp.bfloat16)

    @pl.loop(0, rows // 2)
    def _(n):
        left_row(2 * n)
        left_row(2 * n + 1)

    half = rows // 2
    full = (0, rows, W, W)
    early, late = (0, half, half, W), (half, rows, W, half)

    def column(lhs, c, shape):
        top, bottom, lows, highs = shape
        strip = slice(top * quarter, bottom * quarter)
        at = base + c
        low_l = jnp.concatenate([lhs[at - d, strip] for d in range(1, lows)], axis=1)
        low_r = jnp.concatenate([blocks[at - d, d] for d in range(1, lows)], axis=0)
        high_l = jnp.concatenate([lhs[at + d, strip] for d in range(highs)], axis=1)
        high_r = jnp.concatenate([blocks[at, d] for d in range(highs)], axis=1)
        total = jnp.dot(low_l, low_r, preferred_element_type=jnp.float32)
        total = total + lax.dot_general(
            high_l, high_r, NT, preferred_element_type=jnp.float32
        )
        return [
            (i, total[(i - top) * quarter : (i - top + 1) * quarter]) for i in range(top, bottom)
        ]

    def slot_of(offset):
        return jnp.where((offset >= 0) & (offset < W), offset, W)

    def square_step(c, pieces):
        for i, piece in pieces:
            offset = c - RIM - i
            word = bits[jnp.minimum(c, RIM + i)]
            kept = (lax.shift_right_logical(word, jnp.abs(offset)) & 1) != 0
            filtered[base + c, i * quarter : (i + 1) * quarter, :] = jnp.where(
                kept, piece, 0.0
            ).astype(jnp.bfloat16)
            held[i, slot_of(offset)] = 3.0 * piece

    def cube_step(c, pieces):
        for i, piece in pieces:
            offset = c - RIM - i
            held[i, slot_of(offset)] = held[i, slot_of(offset)] - 2.0 * piece

    def sweep(lo, hi, lhs, body, shape):
        pairs = (hi - lo) // 2

        @pl.loop(0, pairs)
        def _(n):
            c = lo + 2 * n
            one, two = column(lhs, c, shape), column(lhs, c + 1, shape)
            body(c, one)
            body(c + 1, two)

        if (hi - lo) % 2:
            body(jnp.int32(hi - 1), column(lhs, hi - 1, shape))

    sweep(0, half, left, square_step, early)
    sweep(half, span - half, left, square_step, full)
    sweep(span - half, span, left, square_step, late)
    sweep(RIM, RIM + half, filtered, cube_step, (0, half, W, W))
    sweep(RIM + half, span - half, filtered, cube_step, full)
    sweep(span - half, span, filtered, cube_step, late)

    first = r * rows
    for i in range(rows):
        for f in range(out.shape[1]):
            target = targets[f, first + i]
            there = target >= 0
            offset = jnp.where(there, target - first - i, 0)
            out[i, f] = jnp.where(there, held[i, offset], 0.0)


def per_device(row_devices, col_devices, upper_blocks, block_cols, filter_cols):
    rows, kinds, quarter, _ = upper_blocks.shape
    span = rows + 2 * RIM

    vmem = pl.BlockSpec(memory_space=pltpu.VMEM)
    anywhere = pl.BlockSpec(memory_space=pl.ANY)
    window = pl.pallas_call(
        functools.partial(gather_kernel, row_devices, col_devices),
        out_shape=jax.ShapeDtypeStruct((col_devices, span, W, quarter, B), jnp.bfloat16),
        in_specs=[anywhere, anywhere],
        out_specs=anywhere,
        scratch_shapes=[
            pltpu.SMEM((kinds, block_cols.shape[0]), jnp.int32),
            pltpu.VMEM((rows, kinds, quarter, B), jnp.bfloat16),
            pltpu.VMEM((rows, W, quarter, B), jnp.bfloat16),
            pltpu.SemaphoreType.DMA((3,)),
            pltpu.SemaphoreType.DMA((2, col_devices, rows)),
            pltpu.SemaphoreType.DMA((col_devices, rows)),
            pltpu.SemaphoreType.DMA((2, col_devices, rows)),
            pltpu.SemaphoreType.DMA((2, col_devices, rows)),
        ],
        compiler_params=pltpu.CompilerParams(collective_id=0, has_side_effects=True),
        name="gather_window",
    )(block_cols.T, upper_blocks)
    return pl.pallas_call(
        functools.partial(product_kernel, row_devices, rows, quarter),
        out_shape=jax.ShapeDtypeStruct((rows, filter_cols.shape[1], quarter, B), jnp.float32),
        in_specs=[anywhere, anywhere],
        out_specs=vmem,
        scratch_shapes=[
            pltpu.VMEM((span + RIM, W, B, B), jnp.bfloat16),
            pltpu.VMEM((span + 2 * RIM, rows * quarter, B), jnp.bfloat16),
            pltpu.VMEM((span + 2 * RIM, rows * quarter, B), jnp.bfloat16),
            pltpu.VMEM((rows, W + 1, quarter, B), jnp.float32),
            pltpu.SMEM((span,), jnp.int32),
            pltpu.SMEM(filter_cols.shape[::-1], jnp.int32),
            pltpu.SemaphoreType.DMA,
            pltpu.SemaphoreType.DMA((2 + rows, col_devices)),
        ],
        compiler_params=pltpu.CompilerParams(vmem_limit_bytes=60 << 20),
        name="products",
    )(filter_cols.T, window)


def solution(mesh):
    return jax.shard_map(
        functools.partial(per_device, mesh.shape["row"], mesh.shape["col"]),
        mesh=mesh,
        in_specs=(P("row", None, "col", None), P(), P()),
        out_specs=P("row", None, "col", None),
        check_vma=False,
    )
```
